256 devices in a mesh: gz: 4 (over x), gy: 64 (over z, y, core).
Axes of the slice: x: 4, y: 4, z: 8, core: 2. Of those that a mesh axis runs over, the one named last changes fastest.
Arguments:
- velocity_x: bfloat16 [8, 1024, 2048], P('gz', 'gy'), may hold values from -1.5 to 1.5
- velocity_y: bfloat16 [8, 1024, 2048], P('gz', 'gy'), may hold values from -1.5 to 1.5
- velocity_z: bfloat16 [8, 1024, 2048], P('gz', 'gy'), may hold values from -1.5 to 1.5
- owners: int32 [512, 1], replicated, may hold values from 0 to 63; in each aligned block of 512 rows (0 to 511, 512 to 1023, ...) at most 16 rows name the same one
- coupling_below: float32 [8], replicated, may hold values from 0.5 to 2
- coupling_above: float32 [8], replicated, may hold values from 0.5 to 2
- metric: float32 [8], replicated, may hold values from 0.25 to 1
Outputs:
- pressure: float32 [64, 16, 2, 8, 1024], P('gy', None, None, 'gz')
The draws below stay inside these ranges and needn't reach their ends.
Inputs may be any that keep to these rules, and one draw needn't show every extreme that they name: owners[m, 0] is the owner of retained mode kx = m; no owner has more than 16 modes, and some owner has exactly 16.
All inputs are finite; a program needn't handle non-finite values.
Results may differ from the reference program's by a relative error of at most 0.0003.
Values may be sent and summed in bfloat16 or wider, within the bound.
A program may use at most 64 MiB of HBM per device.

```python
import math
import jax
import jax.numpy as jnp
import numpy as np
from jax import lax

NX = 2048
NY = 1024
NZ = 8
KXR = 512
KYR = 1024
CAP = 16
N_GY = 64


def levels(stream_key, extent, shards, low, top_value):
    def one(dim, shards_of):
        steps = jax.random.uniform(jax.random.fold_in(jax.random.fold_in(stream_key, 6), dim), (shards_of,), jnp.float32, low / len(shards), top_value / len(shards))
        return jnp.repeat(jnp.exp(steps), extent[dim] // shards_of).reshape((-1,) + (1,) * (len(extent) - dim - 1))

    level = one(*shards[0])
    for cut in shards[1:]:
        level = level * one(*cut)
    return level


def deal_out(stream_key, own, number, rows, number_of, top, bound, lean):
    order = jax.random.permutation(stream_key, number_of)
    crowded, ordinary = load_shares(number_of, rows * top, bound, lean, True), load_shares(number_of, rows * top, bound, lean, False)
    places = jnp.arange(number_of)

    def named(tallies, rotation):
        used = int((tallies > 0).sum())
        fixed = max(1, used // 4)
        shifted = fixed + (places - fixed + rotation * (used - fixed)) % max(1, number_of - fixed)
        return jnp.zeros((number_of,), jnp.int32).at[order[jnp.where(places < fixed, places, shifted)]].set(jnp.asarray(tallies, jnp.int32))

    tallies = jnp.where(number % 4 == 0, named(crowded, number // 4), named(ordinary, number - number // 4 - 1))
    mixed = jax.random.permutation(jax.random.fold_in(own, 3), number_of)
    source_of, receiver = mixed[0:number_of // 2 * 2:2], mixed[1:number_of // 2 * 2:2]
    margin = jnp.minimum(tallies[source_of] - 1, bound - tallies[receiver]) // 2
    margin = jnp.where((source_of == order[0]) | (receiver == order[0]) | (tallies[receiver] == 0), 0, jnp.maximum(margin, 0))
    shifted = jax.random.randint(jax.random.fold_in(own, 4), (number_of // 2,), 0, 1 << 20) % (margin + 1)
    tallies = tallies.at[source_of].add(-shifted).at[receiver].add(shifted)
    labels = jnp.searchsorted(jnp.cumsum(tallies), jnp.arange(rows * top), side="right").astype(jnp.int32)
    listing = labels.reshape(top, rows).T
    listing = listing[jax.random.permutation(jax.random.fold_in(own, 1), rows)]
    rotation = jax.random.randint(jax.random.fold_in(own, 2), (rows, 1), 0, top)
    return jnp.take_along_axis(listing, (jnp.arange(top)[None, :] + rotation) % top, axis=1)


def load_shares(count, total, bound, skew, full):
    portions = [(1 << 20) // math.isqrt(standing ** skew) + 1 for standing in range(1, count + 1)]
    largest = bound if full else min(bound, max(-(-total // count), total * portions[0] // sum(portions)))
    least = 1 if total - largest >= count - 1 else 0
    holding, surplus = [largest] + [least] * (count - 1), total - largest - least * (count - 1)
    while surplus > 0:
        movable = [i for i in range(1, count) if holding[i] < largest] or [i for i in range(1, count) if holding[i] < bound]
        whole, budget = sum([portions[i] for i in movable]), surplus
        for i in movable:
            more = min(bound - holding[i], max(1, budget * portions[i] // whole), surplus)
            holding[i] = holding[i] + more
            surplus = surplus - more
    return np.array(holding)


def gaussian(key, dims, width, bound, pieces=(), kind=jnp.bfloat16):
    values = jax.random.normal(key, dims, jnp.float32) * width
    if len(pieces) > 0:
        values = levels(key, dims, pieces, -0.22, 0.18) * values
    return jnp.clip(values, min=-bound, max=bound).astype(kind)


def setup_inputs(seed: int = 0) -> dict:
    streams_of = jax.random.split(jax.random.key(seed), 8)
    velocity_x = gaussian(streams_of[0], (NZ, NY, NX), 0.25, 1.5, ((0, 4), (1, 64)))
    velocity_y = gaussian(streams_of[1], (NZ, NY, NX), 0.25, 1.5, ((0, 4), (1, 64)))
    velocity_z = gaussian(streams_of[2], (NZ, NY, NX), 0.25, 1.5, ((0, 4), (1, 64)))
    owners_keys = jax.random.split(jax.random.fold_in(streams_of[3], 1), KXR // KXR)
    owners_turns = jax.random.permutation(jax.random.fold_in(streams_of[3], 3), KXR // KXR)
    owners = jax.vmap(lambda own, number: deal_out(jax.random.fold_in(streams_of[3], 2), own, number, KXR, N_GY, 1, CAP, 1))(owners_keys, owners_turns).reshape((KXR, 1))
    coupling_below = jnp.clip(jnp.exp(jax.random.uniform(streams_of[4], (NZ,), jnp.float32, math.log(0.5), math.log(2.0))), 0.5, 2.0)
    coupling_above = jnp.clip(jnp.exp(jax.random.uniform(streams_of[5], (NZ,), jnp.float32, math.log(0.5), math.log(2.0))), 0.5, 2.0)
    metric = jnp.clip(jnp.exp(jax.random.uniform(streams_of[6], (NZ,), jnp.float32, math.log(0.25), math.log(1.0))), 0.25, 1.0)
    return {"velocity_x": velocity_x, "velocity_y": velocity_y, "velocity_z": velocity_z, "owners": owners, "coupling_below": coupling_below, "coupling_above": coupling_above, "metric": metric}


SMAG_COEF = 0.12
STRAIN_FLOOR = 0.01
BASE_SHIFT = 0.004
MODE_SHIFT = 0.02

def shrink(field):
    return field[1:-1, 1:-1]

def centred_x(field):
    return (jnp.roll(field, -1, 2) - jnp.roll(field, 1, 2)) * 0.5

def slope_x(field):
    return shrink(centred_x(field))

def slope_y(field):
    return (field[1:-1, 2:] - field[1:-1, :-2]) * 0.5

def slope_z(field):
    return (field[2:, 1:-1] - field[:-2, 1:-1]) * 0.5

def second_x(field):
    return shrink(jnp.roll(field, -1, 2) + jnp.roll(field, 1, 2) - 2.0 * field)

def second_y(field):
    return field[1:-1, 2:] + field[1:-1, :-2] - 2.0 * shrink(field)

def second_z(field):
    return field[2:, 1:-1] + field[:-2, 1:-1] - 2.0 * shrink(field)

def mixed_yz(field):
    return 0.25 * (field[2:, 2:] - field[2:, :-2] - field[:-2, 2:] + field[:-2, :-2])

def pressure_source(extended):
    slopes = (slope_x, slope_y, slope_z)
    gradient = [[slopes[axis_two](extended[axis_one]) for axis_two in range(3)] for axis_one in range(3)]
    strain = {}
    for axis_one in range(3):
        for axis_two in range(axis_one, 3):
            strain[axis_one, axis_two] = 0.5 * (gradient[axis_one][axis_two] + gradient[axis_two][axis_one])
    squared = 2.0 * (strain[0, 0] * strain[0, 0] + strain[1, 1] * strain[1, 1] + strain[2, 2] * strain[2, 2])
    squared = squared + 4.0 * (strain[0, 1] * strain[0, 1] + strain[0, 2] * strain[0, 2] + strain[1, 2] * strain[1, 2])
    viscous = 2.0 * SMAG_COEF * jnp.sqrt(squared + STRAIN_FLOOR)
    stress = {}
    for pair_key in strain:
        stress[pair_key] = viscous * strain[pair_key]
    divergence = shrink(gradient[0][0] + gradient[1][1] + gradient[2][2])
    forcing = second_x(stress[0, 0]) + second_y(stress[1, 1]) + second_z(stress[2, 2])
    crossed = slope_y(centred_x(stress[0, 1])) + slope_z(centred_x(stress[0, 2])) + mixed_yz(stress[1, 2])
    return divergence + forcing + 2.0 * crossed

def slot_table(owners, groups, capacity):
    owner_of = owners[:, 0]
    one_hot = (owner_of[:, None] == jnp.arange(groups, dtype=jnp.int32)[None, :]).astype(jnp.int32)
    before = jnp.cumsum(one_hot, axis=0) - one_hot
    rank_in = lax.optimization_barrier(jnp.sum(before * one_hot, axis=1))
    slot_of = owner_of * capacity + rank_in
    matches = slot_of[None, :] == jnp.arange(groups * capacity, dtype=jnp.int32)[:, None]
    mode_ids = jnp.arange(owner_of.shape[0], dtype=jnp.int32)
    slot_mode = lax.optimization_barrier(jnp.sum(jnp.where(matches, mode_ids[None, :], 0), axis=1)).astype(jnp.int32)
    return (slot_mode, jnp.any(matches, axis=1))

def reference(velocity_x, velocity_y, velocity_z, owners, coupling_below, coupling_above, metric):
    stacked = jnp.stack([velocity_x, velocity_y, velocity_z])
    padded = jnp.pad(stacked, ((0, 0), (2, 2), (0, 0), (0, 0)))
    norm_factor = 1.0 / math.sqrt(NX * NY)
    ky_all = jnp.arange(KYR, dtype=jnp.int32) - KXR
    kx_all = jnp.arange(KXR, dtype=jnp.int32)
    ky_rows = jnp.mod(ky_all, NY)
    radius = ky_all[:, None] * ky_all[:, None] + kx_all[None, :] * kx_all[None, :]
    inside = radius <= KXR * KXR

    def one_level(layer_pos):
        slab_data = lax.dynamic_slice_in_dim(padded, layer_pos, 5, 1).astype(jnp.float32)
        slab_data = jnp.pad(slab_data, ((0, 0), (0, 0), (2, 2), (0, 0)))
        source = pressure_source(slab_data)[0]
        spectrum = jnp.fft.rfft(source, axis=1)[:, :KXR]
        spectrum = jnp.fft.fft(spectrum, axis=0)[ky_rows] * norm_factor
        spectrum = jnp.where(inside, spectrum, 0.0)
        return jnp.stack([jnp.real(spectrum), jnp.imag(spectrum)]).astype(jnp.float32)
    spectra = lax.map(one_level, jnp.arange(NZ, dtype=jnp.int32))
    kappa = radius.astype(jnp.float32) / float(KXR * KXR)
    pivots = []
    carried = []
    for layer_pos in range(NZ):
        diagonal = -(coupling_below[layer_pos] + coupling_above[layer_pos] + metric[layer_pos] * (BASE_SHIFT + MODE_SHIFT * kappa))
        rhs_now = spectra[layer_pos]
        if layer_pos == 0:
            pivot = diagonal
            value = rhs_now
        else:
            pivot = diagonal - coupling_below[layer_pos] * coupling_above[layer_pos - 1] / pivots[-1]
            value = rhs_now - coupling_below[layer_pos] * carried[-1] / pivots[-1]
        pivots.append(pivot)
        carried.append(value)
    solution = [None] * NZ
    current = carried[NZ - 1] / pivots[NZ - 1]
    solution[NZ - 1] = current
    for layer_pos in range(NZ - 2, -1, -1):
        current = (carried[layer_pos] - coupling_above[layer_pos] * current) / pivots[layer_pos]
        solution[layer_pos] = current
    field = jnp.stack(solution)
    slot_mode, slot_ok = slot_table(owners, N_GY, CAP)
    picked = jnp.take(field, slot_mode, axis=3)
    picked = jnp.transpose(picked, (3, 1, 0, 2)) * slot_ok[:, None, None, None].astype(jnp.float32)
    return picked.reshape(N_GY, CAP, 2, NZ, KYR)
```

```python
import functools
import math

import jax
import jax.numpy as jnp
import ml_dtypes
import numpy as np
from jax import lax
from jax.experimental import pallas as pl
from jax.experimental.pallas import tpu as pltpu
from jax.sharding import PartitionSpec as P

MESH = pl.DeviceIdType.MESH
F32, BF16, I32 = jnp.float32, jnp.bfloat16, jnp.int32
SMAG_COEF = 0.12
STRAIN_FLOOR = 0.01
BASE_SHIFT = 0.004
MODE_SHIFT = 0.02
NX, NY, NZ, KXR, CAP = 2048, 1024, 8, 512, 16
NGZ, NGY = 4, 64
DEPTH, ROWS = 2, 16
DIAGONAL = ((1, 1), (1, -1), (-1, 1), (-1, -1))


def halves(table):
    high = table.astype(ml_dtypes.bfloat16)
    low = (table - high.astype(np.float64)).astype(ml_dtypes.bfloat16)
    return high, low


def tables():
    a = np.arange(16)
    first = np.zeros((16, 16))
    first[0], first[1] = 1.0, (-1.0) ** a
    for r in range(1, 8):
        first[2 * r] = np.cos(2 * np.pi * ((r * a) % 16) / 16)
        first[2 * r + 1] = -np.sin(2 * np.pi * ((r * a) % 16) / 16)
    spread = np.einsum("ca,rs->crsa", first, np.eye(16)).reshape(256, 256)
    x_first = np.stack(halves(spread))

    b = np.arange(128)
    q = np.arange(32)
    second = np.zeros((8, 2, 128, 2, 2, 32))
    for i in range(8):
        for which, r in enumerate((i, 8 if i == 0 else 16 - i)):
            angle = 2 * np.pi * ((b[:, None] * (16 * q[None, :] + r)) % NX) / NX
            c, s = np.cos(angle), np.sin(angle)
            if i == 0:
                second[i, which, :, 0, which] = c
                second[i, which, :, 1, which] = -s
            else:
                sign = 1.0 if which == 0 else -1.0
                second[i, 0, :, 0, which] = c
                second[i, 1, :, 0, which] = sign * s
                second[i, 0, :, 1, which] = -s
                second[i, 1, :, 1, which] = sign * c
    second = second.reshape(8, 256, 128) / math.sqrt(NX * NY)
    x_second = np.concatenate(halves(second), axis=2)

    s64 = np.arange(64)
    angle = 2 * np.pi * ((s64[:, None] * s64[None, :]) % 64) / 64
    c, s = np.cos(angle), np.sin(angle)
    y_first = np.concatenate([np.concatenate([c, -s], 1), np.concatenate([s, c], 1)], 0)
    y_first = np.concatenate(halves(y_first), axis=1)

    j = np.arange(16)
    angle = 2 * np.pi * (j[:, None] * s64[None, :]) / NY
    c, s = np.cos(angle), np.sin(angle)
    turn = np.stack([np.concatenate([c, c], 1), np.concatenate([s, -s], 1)]).astype(np.float32)

    angle = 2 * np.pi * ((j[:, None] * j[None, :]) % 16) / 16
    both = np.stack([np.cos(angle), np.sin(angle)])
    spread = np.einsum("pqj,xu,yv->pqxyvuj", both, np.eye(2), np.eye(8)).reshape(512, 256)
    y_second = np.concatenate(halves(spread), axis=0)
    return x_first, x_second, y_first, turn, y_second


def split(value):
    high = value.astype(BF16)
    return high, (value - high.astype(F32)).astype(BF16)


def dot(left, right):
    return jnp.dot(left, right, preferred_element_type=F32)


def mode_of(position):
    block, which, q = position // 64, (position // 32) % 2, position % 32
    r = jnp.where(which == 0, block, jnp.where(block == 0, 8, 16 - block))
    return 16 * q + r


def iota(shape, dim):
    return lax.broadcasted_iota(I32, shape, dim)


def next_x(field, ahead):
    if ahead:
        turned = pltpu.roll(field, 127, 2)
        return jnp.where(iota(field.shape, 2) == 127, pltpu.roll(turned, 15, 1), turned)
    turned = pltpu.roll(field, 1, 2)
    return jnp.where(iota(field.shape, 2) == 0, pltpu.roll(turned, 1, 1), turned)


def kernel(
    vx, vy, vz, owners, below, above, metric, x_first_in, x_second_in, y_first_in, turn_in,
    y_second_in, out,
    own, spread, ext, stress, source, outgoing, received, x_first, x_second, y_first, turn,
    y_second, chosen, pivots, edges, edge_in, spectrum,
    in_sem, halo_send, halo_recv, all_send, all_recv, edge_send, edge_recv, own_sem,
):
    gz, gy = lax.axis_index("gz"), lax.axis_index("gy")

    def peer(dz, dy):
        return (lax.rem(gz + dz + NGZ, NGZ), lax.rem(gy + dy + NGY, NGY))

    loads = [pltpu.make_async_copy(v, own.at[i], in_sem.at[i]) for i, v in enumerate((vx, vy, vz))]
    for index, (given, kept) in enumerate(
        ((x_first_in, x_first), (x_second_in, x_second), (y_first_in, y_first), (turn_in, turn),
         (y_second_in, y_second))
    ):
        loads.append(pltpu.make_async_copy(given, kept, in_sem.at[3 + index]))
    for load in loads:
        load.start()

    barrier = pltpu.get_barrier_semaphore()

    @pl.loop(1, NGY)
    def _(d):
        pl.semaphore_signal(barrier, inc=1, device_id=peer(0, d), device_id_type=MESH)

    for d in range(1, NGZ):
        pl.semaphore_signal(barrier, inc=1, device_id=peer(d, 0), device_id_type=MESH)
    for dz, dy in DIAGONAL:
        pl.semaphore_signal(barrier, inc=1, device_id=peer(dz, dy), device_id_type=MESH)

    for c in range(3):
        loads[c].wait()
    for c in range(3):
        for z in range(DEPTH):
            base = (c * DEPTH + z) * ROWS * 16
            for a in range(16):
                spread[pl.ds(base + a, 16, stride=16), :] = own[
                    c, z, :, a * 128 : (a + 1) * 128
                ].astype(F32)
            ext[c, z + 2, 2:18] = spread[base : base + 256, :].reshape(16, 16, 128).astype(BF16)

    pl.semaphore_wait(barrier, NGY - 1 + NGZ - 1 + len(DIAGONAL))

    def level_span(dz):
        return pl.ds({1: 0, 0: 2, -1: 4}[dz], 2)

    def halo(index, dz, dy, levels_from, levels_to):
        rows_from = pl.ds({1: 16, 0: 2, -1: 2}[dy], 16 if dy == 0 else 2)
        rows_to = pl.ds({1: 0, 0: 2, -1: 18}[dy], 16 if dy == 0 else 2)
        return pltpu.make_async_remote_copy(
            src_ref=ext.at[:, levels_from, rows_from],
            dst_ref=ext.at[:, levels_to, rows_to],
            send_sem=halo_send.at[index],
            recv_sem=halo_recv.at[index],
            device_id=peer(dz, dy),
            device_id_type=MESH,
        )

    near = [
        halo(0, 1, 0, pl.ds(3, 1), pl.ds(1, 1)),
        halo(1, -1, 0, pl.ds(2, 1), pl.ds(4, 1)),
        halo(2, 0, 1, level_span(0), level_span(0)),
        halo(3, 0, -1, level_span(0), level_span(0)),
    ]
    for index, (dz, dy) in enumerate(DIAGONAL):
        near.append(halo(4 + index, dz, dy, level_span(0), level_span(dz)))
    far = [halo(8, 1, 0, pl.ds(2, 1), pl.ds(0, 1)), halo(9, -1, 0, pl.ds(3, 1), pl.ds(5, 1))]
    for copy in near + far:
        copy.start()

    owner_row = owners[...]
    kx_row = mode_of(iota((1, KXR), 1))
    named = jnp.where(owner_row == iota((NGY, KXR), 0), 1.0, 0.0).astype(BF16)
    place = jnp.where(iota((KXR, KXR), 0) == kx_row, 1.0, 0.0).astype(BF16)
    named = dot(named, place)
    smaller = jnp.where(mode_of(iota((KXR, 1), 0)) < kx_row, 1.0, 0.0).astype(BF16)
    rank = dot(named.astype(BF16), smaller)
    slot_row = jnp.sum(
        named * (rank + CAP * iota((NGY, KXR), 0).astype(F32)), axis=0, keepdims=True
    ).astype(I32)
    for chi in range(2):
        m = iota((512, 1), 0)
        slot_id = (m // 8) * CAP + chi * 8 + m % 8
        chosen[chi] = jnp.where(slot_row == slot_id, 1.0, 0.0).astype(BF16)
    mine = slot_row == gy * CAP + iota((CAP, KXR), 0)
    own_kx = jnp.sum(jnp.where(mine, kx_row.astype(F32), 0.0), axis=1, keepdims=True)
    own_ok = jnp.sum(jnp.where(mine, 1.0, 0.0), axis=1, keepdims=True)
    ky = (iota((1, NY), 1) - KXR).astype(F32)
    radius = own_kx * own_kx + ky * ky
    inside = jnp.where(radius <= float(KXR * KXR), 1.0, 0.0) * own_ok

    shift = BASE_SHIFT + MODE_SHIFT * (radius / float(KXR * KXR))
    for k in range(NZ):
        pivot = -(below[k] + above[k] + metric[k] * shift)
        if k > 0:
            pivot = pivot - below[k] * above[k - 1] * pivots[2, k - 1]
        pivots[0, k] = pivot
        pivots[2, k] = 1.0 / pivot
    for k in range(NZ - 1, -1, -1):
        pivot = -(below[k] + above[k] + metric[k] * shift)
        if k < NZ - 1:
            pivot = pivot - above[k] * below[k + 1] * pivots[3, k + 1]
        pivots[1, k] = pivot
        pivots[3, k] = 1.0 / pivot

    def zero_rim(levels):
        @pl.when(gy == 0)
        def _():
            for level in levels:
                ext[:, level, 0:2] = jnp.zeros((3, 2, 16, 128), BF16)

        @pl.when(gy == NGY - 1)
        def _():
            for level in levels:
                ext[:, level, 18:20] = jnp.zeros((3, 2, 16, 128), BF16)

    def zero_level(edge, level):
        @pl.when(gz == edge)
        def _():
            for c in range(3):
                ext[c, level] = jnp.zeros((20, 16, 128), BF16)

    def at(c, level, row, count):
        return ext[c, level, pl.ds(row, count)].astype(F32)

    def stress_rows(level, wanted, row, count):
        centre = [at(c, level, row, count) for c in range(3)]
        grad = []
        for c in range(3):
            dx = (next_x(centre[c], True) - next_x(centre[c], False)) * 0.5
            dy = (at(c, level, row + 1, count) - at(c, level, row - 1, count)) * 0.5
            dz = (at(c, level + 1, row, count) - at(c, level - 1, row, count)) * 0.5
            grad.append((dx, dy, dz))
        strain = {
            (i, j): grad[i][i] if i == j else 0.5 * (grad[i][j] + grad[j][i])
            for i in range(3) for j in range(i, 3)
        }
        squared = 2.0 * sum(strain[i, i] * strain[i, i] for i in range(3))
        squared = squared + 4.0 * sum(
            strain[i, j] * strain[i, j] for i in range(3) for j in range(i + 1, 3)
        )
        viscous = 2.0 * SMAG_COEF * jnp.sqrt(squared + STRAIN_FLOOR)
        for index, pair in enumerate(((2, 2), (0, 2), (1, 2), (0, 0), (0, 1), (1, 1))):
            if index < wanted:
                stress[index, level - 1, pl.ds(row - 1, count)] = viscous * strain[pair]

    for copy in near:
        copy.wait_recv()
    zero_level(0, 1)
    zero_level(NGZ - 1, 4)
    zero_rim((1, 2, 3, 4))

    @pl.loop(0, 18)
    def _(step):
        stress_rows(2 + step // 9, 6, 1 + 2 * lax.rem(step, 9), 2)

    for copy in far:
        copy.wait_recv()
    zero_level(0, 0)
    zero_level(NGZ - 1, 5)
    zero_rim((0, 5))

    @pl.loop(0, 18)
    def _(step):
        stress_rows(1 + 3 * (step // 9), 3, 1 + 2 * lax.rem(step, 9), 2)

    for z in range(DEPTH):

        @pl.loop(0, 8)
        def _(step):
            row = 2 * step

            def part(index, dz, dy):
                return stress[index, z + 1 + dz, pl.ds(row + 1 + dy, 2)]

            def wind(c, dz, dy):
                return at(c, z + 2 + dz, row + 2 + dy, 2)

            total = 0.5 * (wind(1, 0, 1) - wind(1, 0, -1) + wind(2, 1, 0) - wind(2, -1, 0))
            total = total + part(5, 0, 1) + part(5, 0, -1) + part(0, 1, 0) + part(0, -1, 0)
            total = total - 2.0 * (part(3, 0, 0) + part(5, 0, 0) + part(0, 0, 0))
            total = total + 0.5 * (
                part(2, 1, 1) - part(2, 1, -1) - part(2, -1, 1) + part(2, -1, -1)
            )
            odd = 0.5 * (
                wind(0, 0, 0) + part(4, 0, 1) - part(4, 0, -1) + part(1, 1, 0) - part(1, -1, 0)
            )
            even = part(3, 0, 0)
            total = total + next_x(even + odd, True) + next_x(even - odd, False)
            high, low = split(total.reshape(32, 128))
            start = pl.multiple_of(32 * step, 32)
            source[0, pl.ds(start, 32), z * 128 : (z + 1) * 128] = high
            source[1, pl.ds(start, 32), z * 128 : (z + 1) * 128] = low

    for load in loads[3:]:
        load.wait()
    high, low = source[0], source[1]
    first = dot(x_first[0], high) + dot(x_first[0], low) + dot(x_first[1], high)
    parts = []
    for i in range(8):
        rows = first[32 * i : 32 * i + 32]
        left = jnp.concatenate(
            [
                jnp.concatenate([rows[0:16, 128 * z : 128 * z + 128], rows[16:32, 128 * z : 128 * z + 128]], 1)
                for z in range(DEPTH)
            ],
            0,
        )
        high, low = split(left)
        both = dot(jnp.concatenate([high, low], 0), x_second[i])
        value = both[0:32, 0:128] + both[32:64, 0:128] + both[0:32, 128:256]
        parts.append(value)
    pieces = []
    for i in range(0, 8, 2):
        one, two = parts[i], parts[i + 1]
        front = iota((32, 128), 1) < 64
        real = jnp.where(front, one, pltpu.roll(two, 64, 1))
        imag = jnp.where(front, pltpu.roll(one, 64, 1), two)
        pieces.append(jnp.concatenate([real, imag], 0))
    modes = jnp.concatenate(pieces, 1)
    high, low = split(modes)
    modes = jnp.concatenate([high, low], 0)
    slots = []
    for chi in range(2):
        taken = lax.dot_general(
            chosen[chi], modes, (((1,), (1,)), ((), ())), preferred_element_type=F32
        )
        slots.append(taken + pltpu.roll(taken, 64, 1))
    together = jnp.where(iota((512, 128), 1) < 64, slots[0], slots[1])
    outgoing[...] = together.reshape(NGY, 8, 128)

    def exchange(d):
        there = lax.rem(gy + d, NGY)
        return pltpu.make_async_remote_copy(
            src_ref=outgoing.at[there],
            dst_ref=received.at[gy],
            send_sem=all_send.at[d],
            recv_sem=all_recv.at[d],
            device_id=(gz, there),
            device_id_type=MESH,
        )

    @pl.loop(1, NGY)
    def _(d):
        exchange(d).start()

    keep = pltpu.make_async_copy(outgoing.at[gy], received.at[gy], own_sem)
    keep.start()
    for copy in near + far:
        copy.wait_send()
    keep.wait()

    @pl.loop(1, NGY)
    def _(d):
        exchange(d).wait()

    rows = []
    flat = received.reshape(NGY * 8, 128)
    for clo in range(8):
        turned = flat[pl.ds(clo, NGY, stride=8), :].T
        for chi in range(2):
            real, imag = turned[64 * chi : 64 * chi + 32], turned[64 * chi + 32 : 64 * chi + 64]
            rows.append(jnp.concatenate([real, imag], 1))
    left = jnp.concatenate(rows, 0)
    high, low = split(left)
    both = dot(jnp.concatenate([high, low], 0), y_first[...])
    value = both[0:512, 0:128] + both[512:1024, 0:128] + both[0:512, 128:256]
    value = value.reshape(32, 16, 128)
    swapped = pltpu.roll(value, 64, 2)
    value = (value * turn[0] + swapped * turn[1]).reshape(16, 2, 16, 128)
    right = jnp.concatenate([value[:, z].reshape(256, 128) for z in range(DEPTH)], 1)
    high, low = split(right)
    by_high = dot(y_second[...], high)
    by_low = dot(y_second[0:512], low)
    both = by_high[0:512] + by_high[512:1024] + by_low
    sign = jnp.where(iota((256, 128), 1) < 64, 1.0, -1.0)
    for z in range(DEPTH):
        lanes = slice(128 * z, 128 * z + 128)
        value = both[0:256, lanes] + pltpu.roll(both[256:512, lanes], 64, 1) * sign
        front = iota((16, 128), 1) < 64
        for pair in range(8):
            one, two = value[32 * pair : 32 * pair + 16], value[32 * pair + 16 : 32 * pair + 32]
            where = slice(128 * ((pair + 4) % 8), 128 * ((pair + 4) % 8) + 128)
            kept = inside[:, where]
            spectrum[0, z, :, where] = jnp.where(front, one, pltpu.roll(two, 64, 1)) * kept
            spectrum[1, z, :, where] = jnp.where(front, pltpu.roll(one, 64, 1), two) * kept

    low_level, high_level = DEPTH * gz, DEPTH * gz + 1
    up = below[high_level] * pivots[2, low_level]
    down = above[low_level] * pivots[3, high_level]
    for part in range(2):
        edges[0, part] = spectrum[part, 1] - up * spectrum[part, 0]
        edges[1, part] = spectrum[part, 0] - down * spectrum[part, 1]

    def edge(d):
        there = lax.rem(gz + d, NGZ)
        side = jnp.where(there > gz, 0, 1)
        return pltpu.make_async_remote_copy(
            src_ref=edges.at[side],
            dst_ref=edge_in.at[gz],
            send_sem=edge_send.at[d],
            recv_sem=edge_recv.at[d],
            device_id=(there, gy),
            device_id_type=MESH,
        )

    for d in range(1, NGZ):
        edge(d).start()
    edge_in[gz] = jnp.zeros((2, CAP, NY), F32)

    first_pivot, last_pivot = pivots[0, low_level], pivots[1, high_level]
    cross_up, cross_down = below[high_level], above[low_level]
    inverse = 1.0 / (first_pivot * last_pivot - cross_up * cross_down)
    beneath = jnp.maximum(low_level - 1, 0)
    over = jnp.minimum(high_level + 1, NZ - 1)
    from_below = below[low_level] * pivots[2, beneath]
    from_above = above[high_level] * pivots[3, over]
    for d in range(1, NGZ):
        edge(d).wait()
    for part in range(2):
        reached = jnp.zeros((CAP, NY), F32)
        for block in range(NGZ - 1):
            new = edge_in[block, part]
            if block > 0:
                k = DEPTH * block
                new = new + (below[k] * below[k + 1]) * pivots[2, k - 1] * pivots[2, k] * reached
            reached = jnp.where(block < gz, new, reached)
        lower = spectrum[part, 0] - from_below * reached
        reached = jnp.zeros((CAP, NY), F32)
        for block in range(NGZ - 1, 0, -1):
            new = edge_in[block, part]
            if block < NGZ - 1:
                k = DEPTH * block
                new = new + (above[k] * above[k + 1]) * pivots[3, k + 1] * pivots[3, k + 2] * reached
            reached = jnp.where(block > gz, new, reached)
        upper = spectrum[part, 1] - from_above * reached
        out[part, 0] = (last_pivot * lower - cross_down * upper) * inverse
        out[part, 1] = (first_pivot * upper - cross_up * lower) * inverse


def per_device(velocity_x, velocity_y, velocity_z, owners, below, above, metric):
    anywhere = pl.BlockSpec(memory_space=pl.ANY)
    scalars = pl.BlockSpec(memory_space=pltpu.SMEM)
    consts = [jnp.asarray(t) for t in tables()]
    dma = pltpu.SemaphoreType.DMA
    result = pl.pallas_call(
        kernel,
        out_shape=jax.ShapeDtypeStruct((2, DEPTH, CAP, NY), F32),
        in_specs=[anywhere] * 3 + [pl.BlockSpec(memory_space=pltpu.VMEM)] + [scalars] * 3 + [anywhere] * 5,
        out_specs=pl.BlockSpec(memory_space=pltpu.VMEM),
        scratch_shapes=[
            pltpu.VMEM((3, DEPTH, ROWS, NX), BF16),
            pltpu.VMEM((3 * DEPTH * ROWS * 16, 128), F32),
            pltpu.VMEM((3, 6, 20, 16, 128), BF16),
            pltpu.VMEM((6, 4, 18, 16, 128), F32),
            pltpu.VMEM((2, 256, 256), BF16),
            pltpu.VMEM((NGY, 8, 128), F32),
            pltpu.VMEM((NGY, 8, 128), F32),
        ]
        + [pltpu.VMEM(c.shape, c.dtype) for c in consts]
        + [
            pltpu.VMEM((2, 512, KXR), BF16),
            pltpu.VMEM((4, NZ, CAP, NY), F32),
            pltpu.VMEM((2, 2, CAP, NY), F32),
            pltpu.VMEM((NGZ, 2, CAP, NY), F32),
            pltpu.VMEM((2, DEPTH, CAP, NY), F32),
            dma((8,)), dma((10,)), dma((10,)), dma((NGY,)), dma((NGY,)), dma((NGZ,)), dma((NGZ,)),
            dma(()),
        ],
        compiler_params=pltpu.CompilerParams(collective_id=0, has_side_effects=True),
    )(velocity_x, velocity_y, velocity_z, owners.reshape(1, KXR), below, above, metric, *consts)
    return jnp.transpose(result, (2, 0, 1, 3))[None]


def solution(mesh):
    placed = (P("gz", "gy", None), P("gz", "gy", None), P("gz", "gy", None), P(), P(), P(), P())
    return jax.shard_map(
        per_device,
        mesh=mesh,
        in_specs=placed,
        out_specs=P("gy", None, None, "gz", None),
        check_vma=False,
    )
```

```python
import functools
import math

import jax
import jax.numpy as jnp
import ml_dtypes
import numpy as np
from jax import lax
from jax.experimental import pallas as pl
from jax.experimental.pallas import tpu as pltpu
from jax.sharding import PartitionSpec as P

MESH = pl.DeviceIdType.MESH
F32, BF16, I32 = jnp.float32, jnp.bfloat16, jnp.int32
SMAG_COEF = 0.12
STRAIN_FLOOR = 0.01
BASE_SHIFT = 0.004
MODE_SHIFT = 0.02
NX, NY, NZ, KXR, CAP = 2048, 1024, 8, 512, 16
NGZ, NGY = 4, 64
DEPTH, ROWS = 2, 16
STRAIGHT = ((1, 0), (-1, 0), (0, 1), (0, -1))
DIAGONAL = ((1, 1), (1, -1), (-1, 1), (-1, -1))


def halves(table):
    high = table.astype(ml_dtypes.bfloat16)
    low = (table - high.astype(np.float64)).astype(ml_dtypes.bfloat16)
    return high, low


def tables():
    a = np.arange(16)
    first = np.zeros((16, 16))
    first[0], first[1] = 1.0, (-1.0) ** a
    for r in range(1, 8):
        first[2 * r] = np.cos(2 * np.pi * ((r * a) % 16) / 16)
        first[2 * r + 1] = -np.sin(2 * np.pi * ((r * a) % 16) / 16)
    spread = np.einsum("ca,rs->crsa", first, np.eye(16)).reshape(256, 256)
    x_first = np.stack(halves(spread))

    b = np.arange(128)
    q = np.arange(32)
    second = np.zeros((8, 2, 128, 2, 2, 32))
    for i in range(8):
        for which, r in enumerate((i, 8 if i == 0 else 16 - i)):
            angle = 2 * np.pi * ((b[:, None] * (16 * q[None, :] + r)) % NX) / NX
            c, s = np.cos(angle), np.sin(angle)
            if i == 0:
                second[i, which, :, 0, which] = c
                second[i, which, :, 1, which] = -s
            else:
                sign = 1.0 if which == 0 else -1.0
                second[i, 0, :, 0, which] = c
                second[i, 1, :, 0, which] = sign * s
                second[i, 0, :, 1, which] = -s
                second[i, 1, :, 1, which] = sign * c
    second = second.reshape(8, 256, 128) / math.sqrt(NX * NY)
    x_second = np.concatenate(halves(second), axis=2)

    s64 = np.arange(64)
    angle = 2 * np.pi * ((s64[:, None] * s64[None, :]) % 64) / 64
    c, s = np.cos(angle), np.sin(angle)
    y_first = np.concatenate([np.concatenate([c, -s], 1), np.concatenate([s, c], 1)], 0)
    y_first = np.concatenate(halves(y_first), axis=1)

    j = np.arange(16)
    angle = 2 * np.pi * (j[:, None] * s64[None, :]) / NY
    c, s = np.cos(angle), np.sin(angle)
    turn = np.stack([np.concatenate([c, c], 1), np.concatenate([s, -s], 1)]).astype(np.float32)

    angle = 2 * np.pi * ((j[:, None] * j[None, :]) % 16) / 16
    both = np.stack([np.cos(angle), np.sin(angle)])
    spread = np.einsum("pqj,xu,yv->pqxyvuj", both, np.eye(2), np.eye(8)).reshape(512, 256)
    y_second = np.concatenate(halves(spread), axis=0)
    return x_first, x_second, y_first, turn, y_second


def split(value):
    high = value.astype(BF16)
    return high, (value - high.astype(F32)).astype(BF16)


def dot(left, right):
    return jnp.dot(left, right, preferred_element_type=F32)


def mode_of(position):
    block, which, q = position // 64, (position // 32) % 2, position % 32
    r = jnp.where(which == 0, block, jnp.where(block == 0, 8, 16 - block))
    return 16 * q + r


def iota(shape, dim):
    return lax.broadcasted_iota(I32, shape, dim)


def next_x(field, ahead):
    if ahead:
        turned = pltpu.roll(field, 127, 2)
        return jnp.where(iota(field.shape, 2) == 127, pltpu.roll(turned, 15, 1), turned)
    turned = pltpu.roll(field, 1, 2)
    return jnp.where(iota(field.shape, 2) == 0, pltpu.roll(turned, 1, 1), turned)


def kernel(
    vx, vy, vz, owners, below, above, metric, x_first_in, x_second_in, y_first_in, turn_in,
    y_second_in, out,
    own, spread, ext, stress, flat, begun, source, outgoing, received, x_first, x_second, y_first, turn,
    y_second, chosen, pivots, edges, edge_in, spectrum,
    in_sem, halo_send, halo_recv, all_send, all_recv, edge_send, edge_recv, own_sem, meeting,
):
    gz, gy = lax.axis_index("gz"), lax.axis_index("gy")

    def peer(dz, dy):
        return (lax.rem(gz + dz + NGZ, NGZ), lax.rem(gy + dy + NGY, NGY))

    loads = [pltpu.make_async_copy(v, own.at[i], in_sem.at[i]) for i, v in enumerate((vx, vy, vz))]
    for index, (given, kept) in enumerate(
        ((x_first_in, x_first), (x_second_in, x_second), (y_first_in, y_first), (turn_in, turn),
         (y_second_in, y_second))
    ):
        loads.append(pltpu.make_async_copy(given, kept, in_sem.at[3 + index]))
    for load in loads:
        load.start()

    barrier = pltpu.get_barrier_semaphore()

    for dz, dy in STRAIGHT + DIAGONAL:
        pl.semaphore_signal(barrier, inc=1, device_id=peer(dz, dy), device_id_type=MESH)

    for c in range(3):
        loads[c].wait()
    for c in range(3):
        for z in range(DEPTH):
            base = (c * DEPTH + z) * ROWS * 16
            for a in range(16):
                spread[pl.ds(base + a, 16, stride=16), :] = own[
                    c, z, :, a * 128 : (a + 1) * 128
                ].astype(F32)
            ext[c, z + 2, 2:18] = spread[base : base + 256, :].reshape(16, 16, 128).astype(BF16)

    pl.semaphore_wait(barrier, len(STRAIGHT) + len(DIAGONAL))

    def copy_to(index, dz, dy, given, kept):
        return pltpu.make_async_remote_copy(
            src_ref=ext.at[:, given[0], given[1]],
            dst_ref=ext.at[:, kept[0], kept[1]],
            send_sem=halo_send.at[index],
            recv_sem=halo_recv.at[index],
            device_id=peer(dz, dy),
            device_id_type=MESH,
        )

    def rows(start, count):
        return pl.ds(start, count)

    near = [
        copy_to(0, 1, 0, (pl.ds(3, 1), rows(2, 16)), (pl.ds(1, 1), rows(2, 16))),
        copy_to(1, -1, 0, (pl.ds(2, 1), rows(2, 16)), (pl.ds(4, 1), rows(2, 16))),
    ]
    rims = [
        copy_to(2, 0, 1, (pl.ds(2, 2), rows(16, 2)), (pl.ds(2, 2), rows(0, 2))),
        copy_to(3, 0, -1, (pl.ds(2, 2), rows(2, 2)), (pl.ds(2, 2), rows(18, 2))),
    ]
    far = [
        copy_to(4, 1, 1, (pl.ds(2, 1), rows(17, 1)), (pl.ds(0, 1), rows(1, 1))),
        copy_to(5, 1, -1, (pl.ds(2, 1), rows(2, 1)), (pl.ds(0, 1), rows(18, 1))),
        copy_to(6, -1, 1, (pl.ds(3, 1), rows(17, 1)), (pl.ds(5, 1), rows(1, 1))),
        copy_to(7, -1, -1, (pl.ds(3, 1), rows(2, 1)), (pl.ds(5, 1), rows(18, 1))),
        copy_to(8, 1, 0, (pl.ds(2, 1), rows(2, 16)), (pl.ds(0, 1), rows(2, 16))),
        copy_to(9, -1, 0, (pl.ds(3, 1), rows(2, 16)), (pl.ds(5, 1), rows(2, 16))),
    ]
    corners = [
        copy_to(10, 0, 1, (pl.ds(1, 1), rows(16, 2)), (pl.ds(1, 1), rows(0, 2))),
        copy_to(11, 0, 1, (pl.ds(4, 1), rows(16, 2)), (pl.ds(4, 1), rows(0, 2))),
        copy_to(12, 0, -1, (pl.ds(1, 1), rows(2, 2)), (pl.ds(1, 1), rows(18, 2))),
        copy_to(13, 0, -1, (pl.ds(4, 1), rows(2, 2)), (pl.ds(4, 1), rows(18, 2))),
    ]
    for copy in near + rims + far:
        copy.start()

    def meet(number, peers):
        for dz, dy in peers:
            pl.semaphore_signal(meeting.at[number], inc=1, device_id=peer(dz, dy), device_id_type=MESH)

    meet(0, STRAIGHT)

    owner_row = owners[...]
    kx_row = mode_of(iota((1, KXR), 1))
    named = jnp.where(owner_row == iota((NGY, KXR), 0), 1.0, 0.0).astype(BF16)
    place = jnp.where(iota((KXR, KXR), 0) == kx_row, 1.0, 0.0).astype(BF16)
    named = dot(named, place)
    smaller = jnp.where(mode_of(iota((KXR, 1), 0)) < kx_row, 1.0, 0.0).astype(BF16)
    rank = dot(named.astype(BF16), smaller)
    slot_row = jnp.sum(
        named * (rank + CAP * iota((NGY, KXR), 0).astype(F32)), axis=0, keepdims=True
    ).astype(I32)
    for chi in range(2):
        m = iota((512, 1), 0)
        slot_id = (m // 8) * CAP + chi * 8 + m % 8
        chosen[chi] = jnp.where(slot_row == slot_id, 1.0, 0.0).astype(BF16)
    mine = slot_row == gy * CAP + iota((CAP, KXR), 0)
    own_kx = jnp.sum(jnp.where(mine, kx_row.astype(F32), 0.0), axis=1, keepdims=True)
    own_ok = jnp.sum(jnp.where(mine, 1.0, 0.0), axis=1, keepdims=True)
    ky = (iota((1, NY), 1) - KXR).astype(F32)
    radius = own_kx * own_kx + ky * ky
    inside = jnp.where(radius <= float(KXR * KXR), 1.0, 0.0) * own_ok

    pl.semaphore_wait(meeting.at[0], len(STRAIGHT))
    meet(1, ((0, 2), (0, -2)))

    shift = BASE_SHIFT + MODE_SHIFT * (radius / float(KXR * KXR))
    for k in range(NZ):
        pivot = -(below[k] + above[k] + metric[k] * shift)
        if k > 0:
            pivot = pivot - below[k] * above[k - 1] * pivots[2, k - 1]
        pivots[0, k] = pivot
        pivots[2, k] = 1.0 / pivot
    for k in range(NZ - 1, -1, -1):
        pivot = -(below[k] + above[k] + metric[k] * shift)
        if k < NZ - 1:
            pivot = pivot - above[k] * below[k + 1] * pivots[3, k + 1]
        pivots[1, k] = pivot
        pivots[3, k] = 1.0 / pivot

    pl.semaphore_wait(meeting.at[1], 2)
    meet(2, ((0, 4), (0, -4)))

    def zero_rim(levels):
        @pl.when(gy == 0)
        def _():
            for level in levels:
                ext[:, level, 0:2] = jnp.zeros((3, 2, 16, 128), BF16)

        @pl.when(gy == NGY - 1)
        def _():
            for level in levels:
                ext[:, level, 18:20] = jnp.zeros((3, 2, 16, 128), BF16)

    def zero_level(edge, level, start, count):
        @pl.when(gz == edge)
        def _():
            for c in range(3):
                ext[c, level, start : start + count] = jnp.zeros((count, 16, 128), BF16)

    def at(c, level, row, count):
        return ext[c, level, pl.ds(row, count)].astype(F32)

    def flat_slopes(level, row, count):
        centre = [at(c, level, row, count) for c in range(3)]
        dx = [(next_x(f, True) - next_x(f, False)) * 0.5 for f in centre]
        dy = [(at(c, level, row + 1, count) - at(c, level, row - 1, count)) * 0.5 for c in range(3)]
        return dx, dy

    def slopes_z(level, row, count):
        return [(at(c, level + 1, row, count) - at(c, level - 1, row, count)) * 0.5 for c in range(3)]

    for copy in near:
        copy.wait_recv()
    zero_level(0, 1, 2, 16)
    zero_level(NGZ - 1, 4, 2, 16)
    for copy in corners:
        copy.start()
    for copy in rims + corners:
        copy.wait_recv()
    for copy in corners:
        copy.wait_send()
    zero_level(0, 1, 0, 20)
    zero_level(NGZ - 1, 4, 0, 20)
    zero_rim((1, 2, 3, 4))

    @pl.loop(0, 18, unroll=3)
    def _(step):
        level, row, count = 2 + step // 9, 1 + 2 * lax.rem(step, 9), 2
        dx, dy = flat_slopes(level, row, count)
        grad = list(zip(dx, dy, slopes_z(level, row, count)))
        strain = {
            (i, j): grad[i][i] if i == j else 0.5 * (grad[i][j] + grad[j][i])
            for i in range(3) for j in range(i, 3)
        }
        squared = 2.0 * sum(strain[i, i] * strain[i, i] for i in range(3))
        squared = squared + 4.0 * sum(
            strain[i, j] * strain[i, j] for i in range(3) for j in range(i + 1, 3)
        )
        viscous = 2.0 * SMAG_COEF * jnp.sqrt(squared + STRAIN_FLOOR)
        for index, pair in enumerate(((2, 2), (0, 2), (1, 2), (0, 0), (0, 1), (1, 1))):
            stress[index, level - 1, pl.ds(row - 1, count)] = viscous * strain[pair]

    pl.semaphore_wait(meeting.at[2], 2)
    meet(3, ((0, 8), (0, -8)))

    @pl.loop(0, 18, unroll=3)
    def _(step):
        side, row, count = step // 9, 1 + 2 * lax.rem(step, 9), 2
        dx, dy = flat_slopes(1 + 3 * side, row, count)
        mixed = 0.5 * (dy[0] + dx[1])
        squared = 2.0 * (dx[0] * dx[0] + dy[1] * dy[1]) + 4.0 * mixed * mixed + STRAIN_FLOOR
        for index, value in enumerate((squared, dx[2], dy[2])):
            flat[index, side, pl.ds(row - 1, count)] = value

    for z in range(DEPTH):

        @pl.loop(0, 8, unroll=4)
        def _(step):
            row = 2 * step
            sign = 1.0 if z == 0 else -1.0

            def part(index, dz, dy):
                return stress[index, z + 1 + dz, pl.ds(row + 1 + dy, 2)]

            def wind(c, dz, dy):
                return at(c, z + 2 + dz, row + 2 + dy, 2)

            beside = 1 - 2 * z
            total = 0.5 * (wind(1, 0, 1) - wind(1, 0, -1) + wind(2, 1, 0) - wind(2, -1, 0))
            total = total + part(5, 0, 1) + part(5, 0, -1) + part(0, beside, 0)
            total = total - 2.0 * (part(3, 0, 0) + part(5, 0, 0) + part(0, 0, 0))
            total = total + (0.5 * sign) * (part(2, beside, 1) - part(2, beside, -1))
            odd = 0.5 * (wind(0, 0, 0) + part(4, 0, 1) - part(4, 0, -1) + sign * part(1, beside, 0))
            even = part(3, 0, 0)
            total = total + next_x(even + odd, True) + next_x(even - odd, False)
            begun[z, pl.ds(row, 2)] = total

    pl.semaphore_wait(meeting.at[3], 2)
    meet(4, ((0, 16), (0, -16)))

    for copy in far:
        copy.wait_recv()
    zero_level(0, 0, 0, 20)
    zero_level(NGZ - 1, 5, 0, 20)
    zero_rim((0, 5))

    @pl.loop(0, 18, unroll=3)
    def _(step):
        side, row, count = step // 9, 1 + 2 * lax.rem(step, 9), 2
        level = 1 + 3 * side
        dz = slopes_z(level, row, count)
        squared, dx_w, dy_w = (flat[index, side, pl.ds(row - 1, count)] for index in range(3))
        strain_x, strain_y = 0.5 * (dz[0] + dx_w), 0.5 * (dz[1] + dy_w)
        squared = squared + 2.0 * dz[2] * dz[2] + 4.0 * (strain_x * strain_x + strain_y * strain_y)
        viscous = 2.0 * SMAG_COEF * jnp.sqrt(squared)
        for index, value in enumerate((dz[2], strain_x, strain_y)):
            stress[index, level - 1, pl.ds(row - 1, count)] = viscous * value

    for z in range(DEPTH):

        @pl.loop(0, 8, unroll=4)
        def _(step):
            row = 2 * step
            sign = -1.0 if z == 0 else 1.0

            def part(index, dy):
                return stress[index, 3 * z, pl.ds(row + 1 + dy, 2)]

            odd = (0.5 * sign) * part(1, 0)
            total = begun[z, pl.ds(row, 2)] + part(0, 0)
            total = total + (0.5 * sign) * (part(2, 1) - part(2, -1))
            total = total + next_x(odd, True) - next_x(odd, False)
            high, low = split(total.reshape(32, 128))
            start = pl.multiple_of(32 * step, 32)
            source[0, pl.ds(start, 32), z * 128 : (z + 1) * 128] = high
            source[1, pl.ds(start, 32), z * 128 : (z + 1) * 128] = low

    for load in loads[3:]:
        load.wait()
    high, low = source[0], source[1]
    first = dot(x_first[0], high) + dot(x_first[0], low) + dot(x_first[1], high)
    parts = []
    for i in range(8):
        lines = first[32 * i : 32 * i + 32]
        left = jnp.concatenate(
            [
                jnp.concatenate(
                    [lines[0:16, 128 * z : 128 * z + 128], lines[16:32, 128 * z : 128 * z + 128]], 1
                )
                for z in range(DEPTH)
            ],
            0,
        )
        high, low = split(left)
        both = dot(jnp.concatenate([high, low], 0), x_second[i])
        value = both[0:32, 0:128] + both[32:64, 0:128] + both[0:32, 128:256]
        parts.append(value)
    pieces = []
    for i in range(0, 8, 2):
        one, two = parts[i], parts[i + 1]
        front = iota((32, 128), 1) < 64
        real = jnp.where(front, one, pltpu.roll(two, 64, 1))
        imag = jnp.where(front, pltpu.roll(one, 64, 1), two)
        pieces.append(jnp.concatenate([real, imag], 0))
    modes = jnp.concatenate(pieces, 1)
    high, low = split(modes)
    modes = jnp.concatenate([high, low], 0)
    slots = []
    for chi in range(2):
        taken = lax.dot_general(
            chosen[chi], modes, (((1,), (1,)), ((), ())), preferred_element_type=F32
        )
        slots.append(taken + pltpu.roll(taken, 64, 1))
    together = jnp.where(iota((512, 128), 1) < 64, slots[0], slots[1])
    outgoing[...] = together.reshape(NGY, 8, 128)

    pl.semaphore_wait(meeting.at[4], 2)

    def exchange(d):
        there = lax.rem(gy + d, NGY)
        return pltpu.make_async_remote_copy(
            src_ref=outgoing.at[there],
            dst_ref=received.at[gy],
            send_sem=all_send.at[d],
            recv_sem=all_recv.at[d],
            device_id=(gz, there),
            device_id_type=MESH,
        )

    @pl.loop(1, NGY)
    def _(d):
        exchange(d).start()

    keep = pltpu.make_async_copy(outgoing.at[gy], received.at[gy], own_sem)
    keep.start()
    for copy in near + rims + far:
        copy.wait_send()
    keep.wait()

    @pl.loop(1, NGY)
    def _(d):
        exchange(d).wait()

    pieces = []
    arrived = received.reshape(NGY * 8, 128)
    for clo in range(8):
        turned = arrived[pl.ds(clo, NGY, stride=8), :].T
        for chi in range(2):
            real, imag = turned[64 * chi : 64 * chi + 32], turned[64 * chi + 32 : 64 * chi + 64]
            pieces.append(jnp.concatenate([real, imag], 1))
    left = jnp.concatenate(pieces, 0)
    high, low = split(left)
    both = dot(jnp.concatenate([high, low], 0), y_first[...])
    value = both[0:512, 0:128] + both[512:1024, 0:128] + both[0:512, 128:256]
    value = value.reshape(32, 16, 128)
    swapped = pltpu.roll(value, 64, 2)
    value = (value * turn[0] + swapped * turn[1]).reshape(16, 2, 16, 128)
    right = jnp.concatenate([value[:, z].reshape(256, 128) for z in range(DEPTH)], 1)
    high, low = split(right)
    by_high = dot(y_second[...], high)
    by_low = dot(y_second[0:512], low)
    both = by_high[0:512] + by_high[512:1024] + by_low
    sign = jnp.where(iota((256, 128), 1) < 64, 1.0, -1.0)
    for z in range(DEPTH):
        lanes = slice(128 * z, 128 * z + 128)
        value = both[0:256, lanes] + pltpu.roll(both[256:512, lanes], 64, 1) * sign
        front = iota((16, 128), 1) < 64
        for pair in range(8):
            one, two = value[32 * pair : 32 * pair + 16], value[32 * pair + 16 : 32 * pair + 32]
            where = slice(128 * ((pair + 4) % 8), 128 * ((pair + 4) % 8) + 128)
            kept = inside[:, where]
            spectrum[0, z, :, where] = jnp.where(front, one, pltpu.roll(two, 64, 1)) * kept
            spectrum[1, z, :, where] = jnp.where(front, pltpu.roll(one, 64, 1), two) * kept

    low_level, high_level = DEPTH * gz, DEPTH * gz + 1
    up = below[high_level] * pivots[2, low_level]
    down = above[low_level] * pivots[3, high_level]
    for part in range(2):
        edges[0, part] = spectrum[part, 1] - up * spectrum[part, 0]
        edges[1, part] = spectrum[part, 0] - down * spectrum[part, 1]

    def edge(d):
        there = lax.rem(gz + d, NGZ)
        side = jnp.where(there > gz, 0, 1)
        return pltpu.make_async_remote_copy(
            src_ref=edges.at[side],
            dst_ref=edge_in.at[gz],
            send_sem=edge_send.at[d],
            recv_sem=edge_recv.at[d],
            device_id=(there, gy),
            device_id_type=MESH,
        )

    for d in range(1, NGZ):
        edge(d).start()
    edge_in[gz] = jnp.zeros((2, CAP, NY), F32)

    first_pivot, last_pivot = pivots[0, low_level], pivots[1, high_level]
    cross_up, cross_down = below[high_level], above[low_level]
    inverse = 1.0 / (first_pivot * last_pivot - cross_up * cross_down)
    beneath = jnp.maximum(low_level - 1, 0)
    over = jnp.minimum(high_level + 1, NZ - 1)
    from_below = below[low_level] * pivots[2, beneath]
    from_above = above[high_level] * pivots[3, over]
    for d in range(1, NGZ):
        edge(d).wait()
    for part in range(2):
        reached = jnp.zeros((CAP, NY), F32)
        for block in range(NGZ - 1):
            new = edge_in[block, part]
            if block > 0:
                k = DEPTH * block
                new = new + (below[k] * below[k + 1]) * pivots[2, k - 1] * pivots[2, k] * reached
            reached = jnp.where(block < gz, new, reached)
        lower = spectrum[part, 0] - from_below * reached
        reached = jnp.zeros((CAP, NY), F32)
        for block in range(NGZ - 1, 0, -1):
            new = edge_in[block, part]
            if block < NGZ - 1:
                k = DEPTH * block
                new = new + (above[k] * above[k + 1]) * pivots[3, k + 1] * pivots[3, k + 2] * reached
            reached = jnp.where(block > gz, new, reached)
        upper = spectrum[part, 1] - from_above * reached
        for z, value in enumerate(
            (last_pivot * lower - cross_down * upper, first_pivot * upper - cross_up * lower)
        ):
            value = value * inverse
            for tile in range(NY // 128):
                out[pl.ds(part * 16 + tile * 2 + z, CAP, stride=32), :] = value[
                    :, tile * 128 : (tile + 1) * 128
                ]


def per_device(velocity_x, velocity_y, velocity_z, owners, below, above, metric):
    anywhere = pl.BlockSpec(memory_space=pl.ANY)
    scalars = pl.BlockSpec(memory_space=pltpu.SMEM)
    consts = [jnp.asarray(t) for t in tables()]
    dma = pltpu.SemaphoreType.DMA
    result = pl.pallas_call(
        kernel,
        out_shape=jax.ShapeDtypeStruct((2 * DEPTH * CAP * NY // 128, 128), F32),
        in_specs=[anywhere] * 3 + [pl.BlockSpec(memory_space=pltpu.VMEM)] + [scalars] * 3 + [anywhere] * 5,
        out_specs=pl.BlockSpec(memory_space=pltpu.VMEM),
        scratch_shapes=[
            pltpu.VMEM((3, DEPTH, ROWS, NX), BF16),
            pltpu.VMEM((3 * DEPTH * ROWS * 16, 128), F32),
            pltpu.VMEM((3, 6, 20, 16, 128), BF16),
            pltpu.VMEM((6, 4, 18, 16, 128), F32),
            pltpu.VMEM((3, 2, 18, 16, 128), F32),
            pltpu.VMEM((DEPTH, ROWS, 16, 128), F32),
            pltpu.VMEM((2, 256, 256), BF16),
            pltpu.VMEM((NGY, 8, 128), F32),
            pltpu.VMEM((NGY, 8, 128), F32),
        ]
        + [pltpu.VMEM(c.shape, c.dtype) for c in consts]
        + [
            pltpu.VMEM((2, 512, KXR), BF16),
            pltpu.VMEM((4, NZ, CAP, NY), F32),
            pltpu.VMEM((2, 2, CAP, NY), F32),
            pltpu.VMEM((NGZ, 2, CAP, NY), F32),
            pltpu.VMEM((2, DEPTH, CAP, NY), F32),
            dma((8,)), dma((14,)), dma((14,)), dma((NGY,)), dma((NGY,)), dma((NGZ,)), dma((NGZ,)),
            dma(()),
            pltpu.SemaphoreType.REGULAR((5,)),
        ],
        compiler_params=pltpu.CompilerParams(collective_id=0, has_side_effects=True),
    )(velocity_x, velocity_y, velocity_z, owners.reshape(1, KXR), below, above, metric, *consts)
    result = result.reshape(CAP, 2, NY // 128, DEPTH, 128)
    return jnp.transpose(result, (0, 1, 3, 2, 4)).reshape(1, CAP, 2, DEPTH, NY)


def solution(mesh):
    placed = (P("gz", "gy", None), P("gz", "gy", None), P("gz", "gy", None), P(), P(), P(), P())
    return jax.shard_map(
        per_device,
        mesh=mesh,
        in_specs=placed,
        out_specs=P("gy", None, None, "gz", None),
        check_vma=False,
    )
```

```python
import functools
import math

import jax
import jax.numpy as jnp
import ml_dtypes
import numpy as np
from jax import lax
from jax.experimental import pallas as pl
from jax.experimental.pallas import tpu as pltpu
from jax.sharding import PartitionSpec as P

MESH = pl.DeviceIdType.MESH
F32, BF16, I32 = jnp.float32, jnp.bfloat16, jnp.int32
SMAG_COEF = 0.12
STRAIN_FLOOR = 0.01
BASE_SHIFT = 0.004
MODE_SHIFT = 0.02
NX, NY, NZ, KXR, CAP = 2048, 1024, 8, 512, 16
NGZ, NGY = 4, 64
DEPTH, ROWS = 2, 16
STRAIGHT = ((1, 0), (-1, 0), (0, 1), (0, -1))
DIAGONAL = ((1, 1), (1, -1), (-1, 1), (-1, -1))


def halves(table):
    high = table.astype(ml_dtypes.bfloat16)
    low = (table - high.astype(np.float64)).astype(ml_dtypes.bfloat16)
    return high, low


def tables():
    a = np.arange(16)
    first = np.zeros((16, 16))
    first[0], first[1] = 1.0, (-1.0) ** a
    for r in range(1, 8):
        first[2 * r] = np.cos(2 * np.pi * ((r * a) % 16) / 16)
        first[2 * r + 1] = -np.sin(2 * np.pi * ((r * a) % 16) / 16)
    spread = np.einsum("ca,rs->crsa", first, np.eye(16)).reshape(256, 256)
    x_first = np.stack(halves(spread))

    b = np.arange(128)
    q = np.arange(32)
    second = np.zeros((8, 2, 128, 2, 2, 32))
    for i in range(8):
        for which, r in enumerate((i, 8 if i == 0 else 16 - i)):
            angle = 2 * np.pi * ((b[:, None] * (16 * q[None, :] + r)) % NX) / NX
            c, s = np.cos(angle), np.sin(angle)
            if i == 0:
                second[i, which, :, 0, which] = c
                second[i, which, :, 1, which] = -s
            else:
                sign = 1.0 if which == 0 else -1.0
                second[i, 0, :, 0, which] = c
                second[i, 1, :, 0, which] = sign * s
                second[i, 0, :, 1, which] = -s
                second[i, 1, :, 1, which] = sign * c
    second = second.reshape(8, 256, 128) / math.sqrt(NX * NY)
    x_second = np.concatenate(halves(second), axis=2)

    s64 = np.arange(64)
    angle = 2 * np.pi * ((s64[:, None] * s64[None, :]) % 64) / 64
    c, s = np.cos(angle), np.sin(angle)
    y_first = np.concatenate([np.concatenate([c, -s], 1), np.concatenate([s, c], 1)], 0)
    y_first = np.concatenate(halves(y_first), axis=1)

    j = np.arange(16)
    angle = 2 * np.pi * (j[:, None] * s64[None, :]) / NY
    c, s = np.cos(angle), np.sin(angle)
    turn = np.stack([np.concatenate([c, c], 1), np.concatenate([s, -s], 1)]).astype(np.float32)

    angle = 2 * np.pi * ((j[:, None] * j[None, :]) % 16) / 16
    both = np.stack([np.cos(angle), np.sin(angle)])
    spread = np.einsum("pqj,xu,yv->pqxyvuj", both, np.eye(2), np.eye(8)).reshape(512, 256)
    y_second = np.concatenate(halves(spread), axis=0)
    return x_first, x_second, y_first, turn, y_second


def split(value):
    high = value.astype(BF16)
    return high, (value - high.astype(F32)).astype(BF16)


def dot(left, right):
    return jnp.dot(left, right, preferred_element_type=F32)


def mode_of(position):
    block, which, q = position // 64, (position // 32) % 2, position % 32
    r = jnp.where(which == 0, block, jnp.where(block == 0, 8, 16 - block))
    return 16 * q + r


def iota(shape, dim):
    return lax.broadcasted_iota(I32, shape, dim)


def next_x(field, ahead):
    if ahead:
        turned = pltpu.roll(field, 127, 2)
        return jnp.where(iota(field.shape, 2) == 127, pltpu.roll(turned, 15, 1), turned)
    turned = pltpu.roll(field, 1, 2)
    return jnp.where(iota(field.shape, 2) == 0, pltpu.roll(turned, 1, 1), turned)


def kernel(
    vx, vy, vz, owners, below, above, metric, x_first_in, x_second_in, y_first_in, turn_in,
    y_second_in, out,
    own, spread, ext, stress, flat, begun, source, outgoing, received, x_first, x_second, y_first, turn,
    y_second, chosen, pivots, edges, edge_in, steps, steps_in, spectrum,
    in_sem, halo_send, halo_recv, all_send, all_recv, edge_send, edge_recv, own_sem, meeting,
):
    gz, gy = lax.axis_index("gz"), lax.axis_index("gy")

    def peer(dz, dy):
        return (lax.rem(gz + dz + NGZ, NGZ), lax.rem(gy + dy + NGY, NGY))

    loads = [pltpu.make_async_copy(v, own.at[i], in_sem.at[i]) for i, v in enumerate((vx, vy, vz))]
    for index, (given, kept) in enumerate(
        ((x_first_in, x_first), (x_second_in, x_second), (y_first_in, y_first), (turn_in, turn),
         (y_second_in, y_second))
    ):
        loads.append(pltpu.make_async_copy(given, kept, in_sem.at[3 + index]))
    for load in loads:
        load.start()

    barrier = pltpu.get_barrier_semaphore()

    for dz, dy in STRAIGHT + DIAGONAL:
        pl.semaphore_signal(barrier, inc=1, device_id=peer(dz, dy), device_id_type=MESH)

    for c in range(3):
        loads[c].wait()
    for c in range(3):
        for z in range(DEPTH):
            base = (c * DEPTH + z) * ROWS * 16
            for a in range(16):
                spread[pl.ds(base + a, 16, stride=16), :] = own[
                    c, z, :, a * 128 : (a + 1) * 128
                ].astype(F32)
            ext[c, z + 2, 2:18] = spread[base : base + 256, :].reshape(16, 16, 128).astype(BF16)

    pl.semaphore_wait(barrier, len(STRAIGHT) + len(DIAGONAL))

    def copy_to(index, dz, dy, given, kept):
        return pltpu.make_async_remote_copy(
            src_ref=ext.at[:, given[0], given[1]],
            dst_ref=ext.at[:, kept[0], kept[1]],
            send_sem=halo_send.at[index],
            recv_sem=halo_recv.at[index],
            device_id=peer(dz, dy),
            device_id_type=MESH,
        )

    def rows(start, count):
        return pl.ds(start, count)

    near = [
        copy_to(0, 1, 0, (pl.ds(3, 1), rows(2, 16)), (pl.ds(1, 1), rows(2, 16))),
        copy_to(1, -1, 0, (pl.ds(2, 1), rows(2, 16)), (pl.ds(4, 1), rows(2, 16))),
    ]
    rims = [
        copy_to(2, 0, 1, (pl.ds(2, 2), rows(16, 2)), (pl.ds(2, 2), rows(0, 2))),
        copy_to(3, 0, -1, (pl.ds(2, 2), rows(2, 2)), (pl.ds(2, 2), rows(18, 2))),
    ]
    far = [
        copy_to(4, 1, 1, (pl.ds(2, 1), rows(17, 1)), (pl.ds(0, 1), rows(1, 1))),
        copy_to(5, 1, -1, (pl.ds(2, 1), rows(2, 1)), (pl.ds(0, 1), rows(18, 1))),
        copy_to(6, -1, 1, (pl.ds(3, 1), rows(17, 1)), (pl.ds(5, 1), rows(1, 1))),
        copy_to(7, -1, -1, (pl.ds(3, 1), rows(2, 1)), (pl.ds(5, 1), rows(18, 1))),
        copy_to(8, 1, 0, (pl.ds(2, 1), rows(2, 16)), (pl.ds(0, 1), rows(2, 16))),
        copy_to(9, -1, 0, (pl.ds(3, 1), rows(2, 16)), (pl.ds(5, 1), rows(2, 16))),
    ]
    corners = [
        copy_to(10, 0, 1, (pl.ds(1, 1), rows(16, 2)), (pl.ds(1, 1), rows(0, 2))),
        copy_to(11, 0, 1, (pl.ds(4, 1), rows(16, 2)), (pl.ds(4, 1), rows(0, 2))),
        copy_to(12, 0, -1, (pl.ds(1, 1), rows(2, 2)), (pl.ds(1, 1), rows(18, 2))),
        copy_to(13, 0, -1, (pl.ds(4, 1), rows(2, 2)), (pl.ds(4, 1), rows(18, 2))),
    ]
    for copy in near + rims + far:
        copy.start()

    def meet(number, peers):
        for dz, dy in peers:
            pl.semaphore_signal(meeting.at[number], inc=1, device_id=peer(dz, dy), device_id_type=MESH)

    meet(0, STRAIGHT)

    owner_row = owners[...]
    kx_row = mode_of(iota((1, KXR), 1))
    named = jnp.where(owner_row == iota((NGY, KXR), 0), 1.0, 0.0).astype(BF16)
    place = jnp.where(iota((KXR, KXR), 0) == kx_row, 1.0, 0.0).astype(BF16)
    named = dot(named, place)
    smaller = jnp.where(mode_of(iota((KXR, 1), 0)) < kx_row, 1.0, 0.0).astype(BF16)
    rank = dot(named.astype(BF16), smaller)
    slot_row = jnp.sum(
        named * (rank + CAP * iota((NGY, KXR), 0).astype(F32)), axis=0, keepdims=True
    ).astype(I32)
    for chi in range(2):
        m = iota((512, 1), 0)
        slot_id = (m // 8) * CAP + chi * 8 + m % 8
        chosen[chi] = jnp.where(slot_row == slot_id, 1.0, 0.0).astype(BF16)
    mine = slot_row == gy * CAP + iota((CAP, KXR), 0)
    own_kx = jnp.sum(jnp.where(mine, kx_row.astype(F32), 0.0), axis=1, keepdims=True)
    own_ok = jnp.sum(jnp.where(mine, 1.0, 0.0), axis=1, keepdims=True)
    ky = (iota((1, NY), 1) - KXR).astype(F32)
    radius = own_kx * own_kx + ky * ky
    inside = jnp.where(radius <= float(KXR * KXR), 1.0, 0.0) * own_ok

    pl.semaphore_wait(meeting.at[0], len(STRAIGHT))
    meet(1, ((0, 2), (0, -2)))

    shift = BASE_SHIFT + MODE_SHIFT * (radius / float(KXR * KXR))
    for k in range(NZ):
        pivot = -(below[k] + above[k] + metric[k] * shift)
        if k > 0:
            pivot = pivot - below[k] * above[k - 1] * pivots[2, k - 1]
        pivots[0, k] = pivot
        pivots[2, k] = 1.0 / pivot
    for k in range(NZ - 1, -1, -1):
        pivot = -(below[k] + above[k] + metric[k] * shift)
        if k < NZ - 1:
            pivot = pivot - above[k] * below[k + 1] * pivots[3, k + 1]
        pivots[1, k] = pivot
        pivots[3, k] = 1.0 / pivot

    pl.semaphore_wait(meeting.at[1], 2)
    meet(2, ((0, 4), (0, -4)))

    def zero_rim(levels):
        @pl.when(gy == 0)
        def _():
            for level in levels:
                ext[:, level, 0:2] = jnp.zeros((3, 2, 16, 128), BF16)

        @pl.when(gy == NGY - 1)
        def _():
            for level in levels:
                ext[:, level, 18:20] = jnp.zeros((3, 2, 16, 128), BF16)

    def zero_level(edge, level, start, count):
        @pl.when(gz == edge)
        def _():
            for c in range(3):
                ext[c, level, start : start + count] = jnp.zeros((count, 16, 128), BF16)

    def at(c, level, row, count):
        return ext[c, level, pl.ds(row, count)].astype(F32)

    def flat_slopes(level, row, count):
        centre = [at(c, level, row, count) for c in range(3)]
        dx = [(next_x(f, True) - next_x(f, False)) * 0.5 for f in centre]
        dy = [(at(c, level, row + 1, count) - at(c, level, row - 1, count)) * 0.5 for c in range(3)]
        return dx, dy

    def slopes_z(level, row, count):
        return [(at(c, level + 1, row, count) - at(c, level - 1, row, count)) * 0.5 for c in range(3)]

    for copy in near:
        copy.wait_recv()
    zero_level(0, 1, 2, 16)
    zero_level(NGZ - 1, 4, 2, 16)
    for copy in corners:
        copy.start()
    for copy in rims + corners:
        copy.wait_recv()
    for copy in corners:
        copy.wait_send()
    zero_level(0, 1, 0, 20)
    zero_level(NGZ - 1, 4, 0, 20)
    zero_rim((1, 2, 3, 4))

    @pl.loop(0, 18, unroll=3)
    def _(step):
        level, row, count = 2 + step // 9, 1 + 2 * lax.rem(step, 9), 2
        dx, dy = flat_slopes(level, row, count)
        grad = list(zip(dx, dy, slopes_z(level, row, count)))
        strain = {
            (i, j): grad[i][i] if i == j else 0.5 * (grad[i][j] + grad[j][i])
            for i in range(3) for j in range(i, 3)
        }
        squared = 2.0 * sum(strain[i, i] * strain[i, i] for i in range(3))
        squared = squared + 4.0 * sum(
            strain[i, j] * strain[i, j] for i in range(3) for j in range(i + 1, 3)
        )
        viscous = 2.0 * SMAG_COEF * jnp.sqrt(squared + STRAIN_FLOOR)
        for index, pair in enumerate(((2, 2), (0, 2), (1, 2), (0, 0), (0, 1), (1, 1))):
            stress[index, level - 1, pl.ds(row - 1, count)] = viscous * strain[pair]

    pl.semaphore_wait(meeting.at[2], 2)
    meet(3, ((0, 8), (0, -8)))

    @pl.loop(0, 18, unroll=3)
    def _(step):
        side, row, count = step // 9, 1 + 2 * lax.rem(step, 9), 2
        dx, dy = flat_slopes(1 + 3 * side, row, count)
        mixed = 0.5 * (dy[0] + dx[1])
        squared = 2.0 * (dx[0] * dx[0] + dy[1] * dy[1]) + 4.0 * mixed * mixed + STRAIN_FLOOR
        for index, value in enumerate((squared, dx[2], dy[2])):
            flat[index, side, pl.ds(row - 1, count)] = value

    for z in range(DEPTH):

        @pl.loop(0, 8, unroll=4)
        def _(step):
            row = 2 * step
            sign = 1.0 if z == 0 else -1.0

            def part(index, dz, dy):
                return stress[index, z + 1 + dz, pl.ds(row + 1 + dy, 2)]

            def wind(c, dz, dy):
                return at(c, z + 2 + dz, row + 2 + dy, 2)

            beside = 1 - 2 * z
            total = 0.5 * (wind(1, 0, 1) - wind(1, 0, -1) + wind(2, 1, 0) - wind(2, -1, 0))
            total = total + part(5, 0, 1) + part(5, 0, -1) + part(0, beside, 0)
            total = total - 2.0 * (part(3, 0, 0) + part(5, 0, 0) + part(0, 0, 0))
            total = total + (0.5 * sign) * (part(2, beside, 1) - part(2, beside, -1))
            odd = 0.5 * (wind(0, 0, 0) + part(4, 0, 1) - part(4, 0, -1) + sign * part(1, beside, 0))
            even = part(3, 0, 0)
            total = total + next_x(even + odd, True) + next_x(even - odd, False)
            begun[z, pl.ds(row, 2)] = total

    pl.semaphore_wait(meeting.at[3], 2)
    meet(4, ((0, 16), (0, -16)))

    for copy in far:
        copy.wait_recv()
    zero_level(0, 0, 0, 20)
    zero_level(NGZ - 1, 5, 0, 20)
    zero_rim((0, 5))

    @pl.loop(0, 18, unroll=3)
    def _(step):
        side, row, count = step // 9, 1 + 2 * lax.rem(step, 9), 2
        level = 1 + 3 * side
        dz = slopes_z(level, row, count)
        squared, dx_w, dy_w = (flat[index, side, pl.ds(row - 1, count)] for index in range(3))
        strain_x, strain_y = 0.5 * (dz[0] + dx_w), 0.5 * (dz[1] + dy_w)
        squared = squared + 2.0 * dz[2] * dz[2] + 4.0 * (strain_x * strain_x + strain_y * strain_y)
        viscous = 2.0 * SMAG_COEF * jnp.sqrt(squared)
        for index, value in enumerate((dz[2], strain_x, strain_y)):
            stress[index, level - 1, pl.ds(row - 1, count)] = viscous * value

    for z in range(DEPTH):

        @pl.loop(0, 8, unroll=4)
        def _(step):
            row = 2 * step
            sign = -1.0 if z == 0 else 1.0

            def part(index, dy):
                return stress[index, 3 * z, pl.ds(row + 1 + dy, 2)]

            odd = (0.5 * sign) * part(1, 0)
            total = begun[z, pl.ds(row, 2)] + part(0, 0)
            total = total + (0.5 * sign) * (part(2, 1) - part(2, -1))
            total = total + next_x(odd, True) - next_x(odd, False)
            high, low = split(total.reshape(32, 128))
            start = pl.multiple_of(32 * step, 32)
            source[0, pl.ds(start, 32), z * 128 : (z + 1) * 128] = high
            source[1, pl.ds(start, 32), z * 128 : (z + 1) * 128] = low

    for load in loads[3:]:
        load.wait()
    high, low = source[0], source[1]
    first = dot(x_first[0], high) + dot(x_first[0], low) + dot(x_first[1], high)
    parts = []
    for i in range(8):
        lines = first[32 * i : 32 * i + 32]
        left = jnp.concatenate(
            [
                jnp.concatenate(
                    [lines[0:16, 128 * z : 128 * z + 128], lines[16:32, 128 * z : 128 * z + 128]], 1
                )
                for z in range(DEPTH)
            ],
            0,
        )
        high, low = split(left)
        both = dot(jnp.concatenate([high, low], 0), x_second[i])
        value = both[0:32, 0:128] + both[32:64, 0:128] + both[0:32, 128:256]
        parts.append(value)
    pieces = []
    for i in range(0, 8, 2):
        one, two = parts[i], parts[i + 1]
        front = iota((32, 128), 1) < 64
        real = jnp.where(front, one, pltpu.roll(two, 64, 1))
        imag = jnp.where(front, pltpu.roll(one, 64, 1), two)
        pieces.append(jnp.concatenate([real, imag], 0))
    modes = jnp.concatenate(pieces, 1)
    high, low = split(modes)
    modes = jnp.concatenate([high, low], 0)
    slots = []
    for chi in range(2):
        taken = lax.dot_general(
            chosen[chi], modes, (((1,), (1,)), ((), ())), preferred_element_type=F32
        )
        slots.append(taken + pltpu.roll(taken, 64, 1))
    together = jnp.where(iota((512, 128), 1) < 64, slots[0], slots[1])
    outgoing[...] = together.reshape(NGY, 8, 128)

    pl.semaphore_wait(meeting.at[4], 2)

    def exchange(given, kept, there):
        return pltpu.make_async_remote_copy(
            src_ref=given,
            dst_ref=kept,
            send_sem=all_send,
            recv_sem=all_recv,
            device_id=(gz, there),
            device_id_type=MESH,
        )

    @pl.loop(0, NGY - 1, unroll=3)
    def _(k):
        there = lax.rem(gy + NGY // 2 + (k + 1) // 2 * (1 - 2 * lax.rem(k, 2)) + NGY, NGY)
        exchange(outgoing.at[there], received.at[gy], there).start()

    keep = pltpu.make_async_copy(outgoing.at[gy], received.at[gy], own_sem)
    keep.start()
    for copy in near + rims + far:
        copy.wait_send()
    keep.wait()

    others = pl.ds(0, NGY - 1)
    exchange(outgoing.at[others], received.at[others], gy).wait()

    pieces = []
    arrived = received.reshape(NGY * 8, 128)
    for clo in range(8):
        turned = arrived[pl.ds(clo, NGY, stride=8), :].T
        for chi in range(2):
            real, imag = turned[64 * chi : 64 * chi + 32], turned[64 * chi + 32 : 64 * chi + 64]
            pieces.append(jnp.concatenate([real, imag], 1))
    left = jnp.concatenate(pieces, 0)
    high, low = split(left)
    both = dot(jnp.concatenate([high, low], 0), y_first[...])
    value = both[0:512, 0:128] + both[512:1024, 0:128] + both[0:512, 128:256]
    value = value.reshape(32, 16, 128)
    swapped = pltpu.roll(value, 64, 2)
    value = (value * turn[0] + swapped * turn[1]).reshape(16, 2, 16, 128)
    right = jnp.concatenate([value[:, z].reshape(256, 128) for z in range(DEPTH)], 1)
    high, low = split(right)
    by_high = dot(y_second[...], high)
    by_low = dot(y_second[0:512], low)
    both = by_high[0:512] + by_high[512:1024] + by_low
    sign = jnp.where(iota((256, 128), 1) < 64, 1.0, -1.0)
    for z in range(DEPTH):
        lanes = slice(128 * z, 128 * z + 128)
        value = both[0:256, lanes] + pltpu.roll(both[256:512, lanes], 64, 1) * sign
        front = iota((16, 128), 1) < 64
        for pair in range(8):
            one, two = value[32 * pair : 32 * pair + 16], value[32 * pair + 16 : 32 * pair + 32]
            where = slice(128 * ((pair + 4) % 8), 128 * ((pair + 4) % 8) + 128)
            kept = inside[:, where]
            spectrum[0, z, :, where] = jnp.where(front, one, pltpu.roll(two, 64, 1)) * kept
            spectrum[1, z, :, where] = jnp.where(front, pltpu.roll(one, 64, 1), two) * kept

    low_level, high_level = DEPTH * gz, DEPTH * gz + 1
    up = below[high_level] * pivots[2, low_level]
    down = above[low_level] * pivots[3, high_level]
    for side in range(2):
        if side == 0:
            values = [spectrum[part, 1] - up * spectrum[part, 0] for part in range(2)]
        else:
            values = [spectrum[part, 0] - down * spectrum[part, 1] for part in range(2)]
        largest = jnp.maximum(jnp.abs(values[0]), jnp.abs(values[1]))
        largest = jnp.maximum(jnp.max(largest, axis=1, keepdims=True), 1e-30)
        scale = 32767.0 / largest
        for part in range(2):
            edges[side, part] = jnp.floor(values[part] * scale + 0.5).astype(I32).astype(jnp.int16)
        steps[side] = jnp.broadcast_to(largest * (1.0 / 32767.0), (CAP, 128))

    def edge(d, given, kept, kind):
        there = lax.rem(gz + d, NGZ)
        return pltpu.make_async_remote_copy(
            src_ref=given.at[jnp.where(there > gz, 0, 1)],
            dst_ref=kept.at[gz],
            send_sem=edge_send.at[kind, d],
            recv_sem=edge_recv.at[kind, d],
            device_id=(there, gy),
            device_id_type=MESH,
        )

    crossing = [
        edge(d, given, kept, kind)
        for d in (2, 1, 3)
        for kind, (given, kept) in enumerate(((edges, edge_in), (steps, steps_in)))
    ]
    for copy in crossing:
        copy.start()
    edge_in[gz] = jnp.zeros((2, CAP, NY), jnp.int16)
    steps_in[gz] = jnp.zeros((CAP, 128), F32)

    first_pivot, last_pivot = pivots[0, low_level], pivots[1, high_level]
    cross_up, cross_down = below[high_level], above[low_level]
    inverse = 1.0 / (first_pivot * last_pivot - cross_up * cross_down)
    beneath = jnp.maximum(low_level - 1, 0)
    over = jnp.minimum(high_level + 1, NZ - 1)
    from_below = below[low_level] * pivots[2, beneath]
    from_above = above[high_level] * pivots[3, over]
    for copy in crossing:
        copy.wait()

    def edge_of(block, part):
        step = jnp.concatenate([steps_in[block]] * (NY // 128), 1)
        return edge_in[block, part].astype(I32).astype(F32) * step

    for part in range(2):
        reached = jnp.zeros((CAP, NY), F32)
        for block in range(NGZ - 1):
            new = edge_of(block, part)
            if block > 0:
                k = DEPTH * block
                new = new + (below[k] * below[k + 1]) * pivots[2, k - 1] * pivots[2, k] * reached
            reached = jnp.where(block < gz, new, reached)
        lower = spectrum[part, 0] - from_below * reached
        reached = jnp.zeros((CAP, NY), F32)
        for block in range(NGZ - 1, 0, -1):
            new = edge_of(block, part)
            if block < NGZ - 1:
                k = DEPTH * block
                new = new + (above[k] * above[k + 1]) * pivots[3, k + 1] * pivots[3, k + 2] * reached
            reached = jnp.where(block > gz, new, reached)
        upper = spectrum[part, 1] - from_above * reached
        for z, value in enumerate(
            (last_pivot * lower - cross_down * upper, first_pivot * upper - cross_up * lower)
        ):
            value = value * inverse
            for tile in range(NY // 128):
                out[pl.ds(part * 16 + tile * 2 + z, CAP, stride=32), :] = value[
                    :, tile * 128 : (tile + 1) * 128
                ]


def per_device(velocity_x, velocity_y, velocity_z, owners, below, above, metric):
    anywhere = pl.BlockSpec(memory_space=pl.ANY)
    scalars = pl.BlockSpec(memory_space=pltpu.SMEM)
    consts = [jnp.asarray(t) for t in tables()]
    dma = pltpu.SemaphoreType.DMA
    result = pl.pallas_call(
        kernel,
        out_shape=pltpu.VMEM((2 * DEPTH * CAP * NY // 128, 128), F32),
        in_specs=[anywhere] * 3 + [pl.BlockSpec(memory_space=pltpu.VMEM)] + [scalars] * 3 + [anywhere] * 5,
        out_specs=pl.BlockSpec(memory_space=pltpu.VMEM),
        scratch_shapes=[
            pltpu.VMEM((3, DEPTH, ROWS, NX), BF16),
            pltpu.VMEM((3 * DEPTH * ROWS * 16, 128), F32),
            pltpu.VMEM((3, 6, 20, 16, 128), BF16),
            pltpu.VMEM((6, 4, 18, 16, 128), F32),
            pltpu.VMEM((3, 2, 18, 16, 128), F32),
            pltpu.VMEM((DEPTH, ROWS, 16, 128), F32),
            pltpu.VMEM((2, 256, 256), BF16),
            pltpu.VMEM((NGY, 8, 128), F32),
            pltpu.VMEM((NGY, 8, 128), F32),
        ]
        + [pltpu.VMEM(c.shape, c.dtype) for c in consts]
        + [
            pltpu.VMEM((2, 512, KXR), BF16),
            pltpu.VMEM((4, NZ, CAP, NY), F32),
            pltpu.VMEM((2, 2, CAP, NY), jnp.int16),
            pltpu.VMEM((NGZ, 2, CAP, NY), jnp.int16),
            pltpu.VMEM((2, CAP, 128), F32),
            pltpu.VMEM((NGZ, CAP, 128), F32),
            pltpu.VMEM((2, DEPTH, CAP, NY), F32),
            dma((8,)), dma((14,)), dma((14,)), dma(()), dma(()), dma((2, NGZ)), dma((2, NGZ)),
            dma(()),
            pltpu.SemaphoreType.REGULAR((5,)),
        ],
        compiler_params=pltpu.CompilerParams(collective_id=0, has_side_effects=True),
    )(velocity_x, velocity_y, velocity_z, owners.reshape(1, KXR), below, above, metric, *consts)
    result = result.reshape(CAP, 2, NY // 128, DEPTH, 128)
    return jnp.transpose(result, (0, 1, 3, 2, 4)).reshape(1, CAP, 2, DEPTH, NY)


def solution(mesh):
    placed = (P("gz", "gy", None), P("gz", "gy", None), P("gz", "gy", None), P(), P(), P(), P())
    return jax.shard_map(
        per_device,
        mesh=mesh,
        in_specs=placed,
        out_specs=P("gy", None, None, "gz", None),
        check_vma=False,
    )
```

```python
import functools
import math

import jax
import jax.numpy as jnp
import ml_dtypes
import numpy as np
from jax import lax
from jax.experimental import pallas as pl
from jax.experimental.pallas import tpu as pltpu
from jax.sharding import PartitionSpec as P

MESH = pl.DeviceIdType.MESH
F32, BF16, I32 = jnp.float32, jnp.bfloat16, jnp.int32
SMAG_COEF = 0.12
STRAIN_FLOOR = 0.01
BASE_SHIFT = 0.004
MODE_SHIFT = 0.02
NX, NY, NZ, KXR, CAP = 2048, 1024, 8, 512, 16
NGZ, NGY = 4, 64
DEPTH, ROWS = 2, 16
STRAIGHT = ((1, 0), (-1, 0), (0, 1), (0, -1))


def halves(table):
    high = table.astype(ml_dtypes.bfloat16)
    low = (table - high.astype(np.float64)).astype(ml_dtypes.bfloat16)
    return high, low


def tables():
    a = np.arange(16)
    first = np.zeros((16, 16))
    first[0], first[1] = 1.0, (-1.0) ** a
    for r in range(1, 8):
        first[2 * r] = np.cos(2 * np.pi * ((r * a) % 16) / 16)
        first[2 * r + 1] = -np.sin(2 * np.pi * ((r * a) % 16) / 16)
    spread = np.einsum("ca,rs->crsa", first, np.eye(16)).reshape(256, 256)
    x_first = np.stack(halves(spread))

    b = np.arange(128)
    q = np.arange(32)
    second = np.zeros((8, 2, 128, 2, 2, 32))
    for i in range(8):
        for which, r in enumerate((i, 8 if i == 0 else 16 - i)):
            angle = 2 * np.pi * ((b[:, None] * (16 * q[None, :] + r)) % NX) / NX
            c, s = np.cos(angle), np.sin(angle)
            if i == 0:
                second[i, which, :, 0, which] = c
                second[i, which, :, 1, which] = -s
            else:
                sign = 1.0 if which == 0 else -1.0
                second[i, 0, :, 0, which] = c
                second[i, 1, :, 0, which] = sign * s
                second[i, 0, :, 1, which] = -s
                second[i, 1, :, 1, which] = sign * c
    second = second.reshape(8, 256, 128) / math.sqrt(NX * NY)
    x_second = np.concatenate(halves(second), axis=2)

    s64 = np.arange(64)
    angle = 2 * np.pi * ((s64[:, None] * s64[None, :]) % 64) / 64
    c, s = np.cos(angle), np.sin(angle)
    y_first = np.concatenate([np.concatenate([c, -s], 1), np.concatenate([s, c], 1)], 0)
    y_first = np.concatenate(halves(y_first), axis=1)

    j = np.arange(16)
    angle = 2 * np.pi * (j[:, None] * s64[None, :]) / NY
    c, s = np.cos(angle), np.sin(angle)
    turn = np.stack([np.concatenate([c, c], 1), np.concatenate([s, -s], 1)]).astype(np.float32)

    angle = 2 * np.pi * ((j[:, None] * j[None, :]) % 16) / 16
    both = np.stack([np.cos(angle), np.sin(angle)])
    spread = np.einsum("pqj,yv->pqyvj", both, np.eye(8)).reshape(256, 128)
    y_second = np.concatenate(halves(spread), axis=0)
    return x_first, x_second, y_first, turn, y_second


def split(value):
    high = value.astype(BF16)
    return high, (value - high.astype(F32)).astype(BF16)


def dot(left, right):
    return jnp.dot(left, right, preferred_element_type=F32)


def mode_of(position):
    block, which, q = position // 64, (position // 32) % 2, position % 32
    r = jnp.where(which == 0, block, jnp.where(block == 0, 8, 16 - block))
    return 16 * q + r


def iota(shape, dim):
    return lax.broadcasted_iota(I32, shape, dim)


def next_x(field, ahead):
    if ahead:
        turned = pltpu.roll(field, 127, 2)
        return jnp.where(iota(field.shape, 2) == 127, pltpu.roll(turned, 15, 1), turned)
    turned = pltpu.roll(field, 1, 2)
    return jnp.where(iota(field.shape, 2) == 0, pltpu.roll(turned, 1, 1), turned)


def kernel(
    vx, vy, vz, owners_in, below, above, metric, x_first_in, x_second_in, y_first_in, turn_in,
    y_second_in, out,
    own, owners, spread, ext, stress, flat, begun, source, outgoing, received, x_first, x_second, y_first, turn,
    y_second, chosen, pivots, edges, edge_in, steps, steps_in, spectrum,
    in_sem, halo_send, halo_recv, all_send, all_recv, edge_send, edge_recv, own_sem, meeting,
):
    gz, gy = lax.axis_index("gz"), lax.axis_index("gy")

    def peer(dz, dy):
        return (lax.rem(gz + dz + NGZ, NGZ), lax.rem(gy + dy + NGY, NGY))

    loads = [pltpu.make_async_copy(v, own.at[i], in_sem.at[i]) for i, v in enumerate((vx, vy, vz))]
    for index, (given, kept) in enumerate(
        ((owners_in, owners), (x_first_in, x_first), (x_second_in, x_second), (y_first_in, y_first), (turn_in, turn),
         (y_second_in, y_second))
    ):
        loads.append(pltpu.make_async_copy(given, kept, in_sem.at[3 + index]))
    for load in loads:
        load.start()

    barrier = pltpu.get_barrier_semaphore()

    for dz, dy in STRAIGHT:
        pl.semaphore_signal(barrier, inc=1, device_id=peer(dz, dy), device_id_type=MESH)

    for c in range(3):
        loads[c].wait()
    for c in range(3):
        for z in range(DEPTH):
            base = (c * DEPTH + z) * ROWS * 16
            for a in range(16):
                spread[pl.ds(base + a, 16, stride=16), :] = own[
                    c, z, :, a * 128 : (a + 1) * 128
                ].astype(F32)
            ext[c, z + 2, 2:18] = spread[base : base + 256, :].reshape(16, 16, 128).astype(BF16)

    pl.semaphore_wait(barrier, len(STRAIGHT))

    def copy_to(index, dz, dy, given, kept):
        return pltpu.make_async_remote_copy(
            src_ref=ext.at[:, given[0], given[1]],
            dst_ref=ext.at[:, kept[0], kept[1]],
            send_sem=halo_send.at[index],
            recv_sem=halo_recv.at[index],
            device_id=peer(dz, dy),
            device_id_type=MESH,
        )

    def rows(start, count):
        return pl.ds(start, count)

    near = [
        copy_to(0, 1, 0, (pl.ds(3, 1), rows(2, 16)), (pl.ds(1, 1), rows(2, 16))),
        copy_to(1, -1, 0, (pl.ds(2, 1), rows(2, 16)), (pl.ds(4, 1), rows(2, 16))),
    ]
    rims = [
        copy_to(2, 0, 1, (pl.ds(2, 2), rows(16, 2)), (pl.ds(2, 2), rows(0, 2))),
        copy_to(3, 0, -1, (pl.ds(2, 2), rows(2, 2)), (pl.ds(2, 2), rows(18, 2))),
    ]
    far = [
        copy_to(4, 1, 1, (pl.ds(2, 1), rows(17, 1)), (pl.ds(0, 1), rows(1, 1))),
        copy_to(5, 1, -1, (pl.ds(2, 1), rows(2, 1)), (pl.ds(0, 1), rows(18, 1))),
        copy_to(6, -1, 1, (pl.ds(3, 1), rows(17, 1)), (pl.ds(5, 1), rows(1, 1))),
        copy_to(7, -1, -1, (pl.ds(3, 1), rows(2, 1)), (pl.ds(5, 1), rows(18, 1))),
        copy_to(8, 1, 0, (pl.ds(2, 1), rows(2, 16)), (pl.ds(0, 1), rows(2, 16))),
        copy_to(9, -1, 0, (pl.ds(3, 1), rows(2, 16)), (pl.ds(5, 1), rows(2, 16))),
    ]
    corners = [
        copy_to(10, 0, 1, (pl.ds(1, 1), rows(16, 2)), (pl.ds(1, 1), rows(0, 2))),
        copy_to(11, 0, 1, (pl.ds(4, 1), rows(16, 2)), (pl.ds(4, 1), rows(0, 2))),
        copy_to(12, 0, -1, (pl.ds(1, 1), rows(2, 2)), (pl.ds(1, 1), rows(18, 2))),
        copy_to(13, 0, -1, (pl.ds(4, 1), rows(2, 2)), (pl.ds(4, 1), rows(18, 2))),
    ]
    for copy in near + rims:
        copy.start()

    def meet(number, peers):
        for dz, dy in peers:
            pl.semaphore_signal(meeting.at[number], inc=1, device_id=peer(dz, dy), device_id_type=MESH)

    meet(0, STRAIGHT)
    pl.semaphore_wait(meeting.at[0], len(STRAIGHT))
    for copy in far:
        copy.start()
    meet(1, ((0, 2), (0, -2)))

    loads[3].wait()
    owner_row = owners[...]
    kx_row = mode_of(iota((1, KXR), 1))
    named = jnp.where(owner_row == iota((NGY, KXR), 0), 1.0, 0.0).astype(BF16)
    place = jnp.where(iota((KXR, KXR), 0) == kx_row, 1.0, 0.0).astype(BF16)
    named = dot(named, place)
    smaller = jnp.where(mode_of(iota((KXR, 1), 0)) < kx_row, 1.0, 0.0).astype(BF16)
    rank = dot(named.astype(BF16), smaller)
    slot_row = jnp.sum(
        named * (rank + CAP * iota((NGY, KXR), 0).astype(F32)), axis=0, keepdims=True
    ).astype(I32)
    for k in range(4):
        m = iota((256, 1), 0)
        slot_id = (m // 4) * CAP + k * 4 + m % 4
        chosen[k] = jnp.where(slot_row == slot_id, 1.0, 0.0).astype(BF16)
    mine = slot_row == gy * CAP + iota((CAP, KXR), 0)
    own_kx = jnp.sum(jnp.where(mine, kx_row.astype(F32), 0.0), axis=1, keepdims=True)
    own_ok = jnp.sum(jnp.where(mine, 1.0, 0.0), axis=1, keepdims=True)
    ky = (iota((1, NY), 1) - KXR).astype(F32)
    radius = own_kx * own_kx + ky * ky
    inside = jnp.where(radius <= float(KXR * KXR), 1.0, 0.0) * own_ok


    shift = BASE_SHIFT + MODE_SHIFT * (radius / float(KXR * KXR))
    for k in range(NZ):
        pivot = -(below[k] + above[k] + metric[k] * shift)
        if k > 0:
            pivot = pivot - below[k] * above[k - 1] * pivots[2, k - 1]
        pivots[0, k] = pivot
        pivots[2, k] = 1.0 / pivot
    for k in range(NZ - 1, -1, -1):
        pivot = -(below[k] + above[k] + metric[k] * shift)
        if k < NZ - 1:
            pivot = pivot - above[k] * below[k + 1] * pivots[3, k + 1]
        pivots[1, k] = pivot
        pivots[3, k] = 1.0 / pivot

    pl.semaphore_wait(meeting.at[1], 2)
    meet(2, ((0, 4), (0, -4)))

    def zero_rim(levels):
        @pl.when(gy == 0)
        def _():
            for level in levels:
                ext[:, level, 0:2] = jnp.zeros((3, 2, 16, 128), BF16)

        @pl.when(gy == NGY - 1)
        def _():
            for level in levels:
                ext[:, level, 18:20] = jnp.zeros((3, 2, 16, 128), BF16)

    def zero_level(edge, level, start, count):
        @pl.when(gz == edge)
        def _():
            for c in range(3):
                ext[c, level, start : start + count] = jnp.zeros((count, 16, 128), BF16)

    def at(c, level, row, count):
        return ext[c, level, pl.ds(row, count)].astype(F32)

    def flat_slopes(level, row, count):
        centre = [at(c, level, row, count) for c in range(3)]
        dx = [(next_x(f, True) - next_x(f, False)) * 0.5 for f in centre]
        dy = [(at(c, level, row + 1, count) - at(c, level, row - 1, count)) * 0.5 for c in range(3)]
        return dx, dy

    def slopes_z(level, row, count):
        return [(at(c, level + 1, row, count) - at(c, level - 1, row, count)) * 0.5 for c in range(3)]

    for copy in near:
        copy.wait_recv()
    zero_level(0, 1, 2, 16)
    zero_level(NGZ - 1, 4, 2, 16)
    for copy in corners:
        copy.start()
    for copy in rims + corners:
        copy.wait_recv()
    for copy in corners:
        copy.wait_send()
    zero_level(0, 1, 0, 20)
    zero_level(NGZ - 1, 4, 0, 20)
    zero_rim((1, 2, 3, 4))

    @pl.loop(0, 18, unroll=3)
    def _(step):
        level, row, count = 2 + step // 9, 1 + 2 * lax.rem(step, 9), 2
        dx, dy = flat_slopes(level, row, count)
        grad = list(zip(dx, dy, slopes_z(level, row, count)))
        strain = {
            (i, j): grad[i][i] if i == j else 0.5 * (grad[i][j] + grad[j][i])
            for i in range(3) for j in range(i, 3)
        }
        squared = 2.0 * sum(strain[i, i] * strain[i, i] for i in range(3))
        squared = squared + 4.0 * sum(
            strain[i, j] * strain[i, j] for i in range(3) for j in range(i + 1, 3)
        )
        viscous = 2.0 * SMAG_COEF * jnp.sqrt(squared + STRAIN_FLOOR)
        for index, pair in enumerate(((2, 2), (0, 2), (1, 2), (0, 0), (0, 1), (1, 1))):
            stress[index, level - 1, pl.ds(row - 1, count)] = viscous * strain[pair]

    pl.semaphore_wait(meeting.at[2], 2)
    meet(3, ((0, 8), (0, -8)))

    @pl.loop(0, 18, unroll=3)
    def _(step):
        side, row, count = step // 9, 1 + 2 * lax.rem(step, 9), 2
        dx, dy = flat_slopes(1 + 3 * side, row, count)
        mixed = 0.5 * (dy[0] + dx[1])
        squared = 2.0 * (dx[0] * dx[0] + dy[1] * dy[1]) + 4.0 * mixed * mixed + STRAIN_FLOOR
        for index, value in enumerate((squared, dx[2], dy[2])):
            flat[index, side, pl.ds(row - 1, count)] = value

    for z in range(DEPTH):

        @pl.loop(0, 8, unroll=4)
        def _(step):
            row = 2 * step
            sign = 1.0 if z == 0 else -1.0

            def part(index, dz, dy):
                return stress[index, z + 1 + dz, pl.ds(row + 1 + dy, 2)]

            def wind(c, dz, dy):
                return at(c, z + 2 + dz, row + 2 + dy, 2)

            beside = 1 - 2 * z
            total = 0.5 * (wind(1, 0, 1) - wind(1, 0, -1) + wind(2, 1, 0) - wind(2, -1, 0))
            total = total + part(5, 0, 1) + part(5, 0, -1) + part(0, beside, 0)
            total = total - 2.0 * (part(3, 0, 0) + part(5, 0, 0) + part(0, 0, 0))
            total = total + (0.5 * sign) * (part(2, beside, 1) - part(2, beside, -1))
            odd = 0.5 * (wind(0, 0, 0) + part(4, 0, 1) - part(4, 0, -1) + sign * part(1, beside, 0))
            even = part(3, 0, 0)
            total = total + next_x(even + odd, True) + next_x(even - odd, False)
            begun[z, pl.ds(row, 2)] = total

    pl.semaphore_wait(meeting.at[3], 2)
    meet(4, ((0, 16), (0, -16)))

    for copy in far:
        copy.wait_recv()
    zero_level(0, 0, 0, 20)
    zero_level(NGZ - 1, 5, 0, 20)
    zero_rim((0, 5))

    @pl.loop(0, 18, unroll=3)
    def _(step):
        side, row, count = step // 9, 1 + 2 * lax.rem(step, 9), 2
        level = 1 + 3 * side
        dz = slopes_z(level, row, count)
        squared, dx_w, dy_w = (flat[index, side, pl.ds(row - 1, count)] for index in range(3))
        strain_x, strain_y = 0.5 * (dz[0] + dx_w), 0.5 * (dz[1] + dy_w)
        squared = squared + 2.0 * dz[2] * dz[2] + 4.0 * (strain_x * strain_x + strain_y * strain_y)
        viscous = 2.0 * SMAG_COEF * jnp.sqrt(squared)
        for index, value in enumerate((dz[2], strain_x, strain_y)):
            stress[index, level - 1, pl.ds(row - 1, count)] = viscous * value

    for z in range(DEPTH):

        @pl.loop(0, 8, unroll=4)
        def _(step):
            row = 2 * step
            sign = -1.0 if z == 0 else 1.0

            def part(index, dy):
                return stress[index, 3 * z, pl.ds(row + 1 + dy, 2)]

            odd = (0.5 * sign) * part(1, 0)
            total = begun[z, pl.ds(row, 2)] + part(0, 0)
            total = total + (0.5 * sign) * (part(2, 1) - part(2, -1))
            total = total + next_x(odd, True) - next_x(odd, False)
            high, low = split(total.reshape(32, 128))
            start = pl.multiple_of(32 * step, 32)
            source[0, pl.ds(start, 32), z * 128 : (z + 1) * 128] = high
            source[1, pl.ds(start, 32), z * 128 : (z + 1) * 128] = low

    for load in loads[4:]:
        load.wait()
    high, low = source[0], source[1]
    first = dot(x_first[0], high) + dot(x_first[0], low) + dot(x_first[1], high)
    parts = []
    for i in range(8):
        lines = first[32 * i : 32 * i + 32]
        left = jnp.concatenate(
            [
                jnp.concatenate(
                    [lines[0:16, 128 * z : 128 * z + 128], lines[16:32, 128 * z : 128 * z + 128]], 1
                )
                for z in range(DEPTH)
            ],
            0,
        )
        high, low = split(left)
        both = dot(jnp.concatenate([high, low], 0), x_second[i])
        value = both[0:32, 0:128] + both[32:64, 0:128] + both[0:32, 128:256]
        parts.append(value)
    pieces = []
    for i in range(0, 8, 2):
        one, two = parts[i], parts[i + 1]
        front = iota((32, 128), 1) < 64
        real = jnp.where(front, one, pltpu.roll(two, 64, 1))
        imag = jnp.where(front, pltpu.roll(one, 64, 1), two)
        pieces.append(jnp.concatenate([real, imag], 0))
    modes = jnp.concatenate(pieces, 1)
    high, low = split(modes)
    modes = jnp.concatenate([high, low], 0)
    slots = []
    for k in range(4):
        taken = lax.dot_general(
            chosen[k], modes, (((1,), (1,)), ((), ())), preferred_element_type=F32
        )
        slots.append(taken + pltpu.roll(taken, 64, 1))
    front = iota((256, 128), 1) < 64
    low, high = jnp.where(front, slots[0], slots[2]), jnp.where(front, slots[1], slots[3])
    largest = jnp.max(jnp.maximum(jnp.abs(low), jnp.abs(high)), axis=0, keepdims=True)
    exponent = jnp.ceil(jnp.log2(jnp.maximum(largest, 1e-30)) * 64.0) + 1.0
    scale = 32767.0 * jnp.exp2(exponent * (-1.0 / 64.0))
    low, high = (jnp.floor(v * scale + 0.5).astype(I32) for v in (low, high))
    words = (high << 16) | (low & 0xFFFF)
    for g in range(NGY):
        outgoing[g, 0:4] = words[4 * g : 4 * g + 4]
    outgoing[:, 4:5] = jnp.broadcast_to(exponent.astype(I32)[None], (NGY, 1, 128))

    pl.semaphore_wait(meeting.at[4], 2)

    def exchange(given, kept, there):
        return pltpu.make_async_remote_copy(
            src_ref=given,
            dst_ref=kept,
            send_sem=all_send,
            recv_sem=all_recv,
            device_id=(gz, there),
            device_id_type=MESH,
        )

    @pl.loop(0, NGY - 1, unroll=3)
    def _(k):
        there = lax.rem(gy + NGY // 2 + (k + 1) // 2 * (1 - 2 * lax.rem(k, 2)) + NGY, NGY)
        exchange(outgoing.at[there, 0:5], received.at[gy, 0:5], there).start()

    keep = pltpu.make_async_copy(outgoing.at[gy, 0:5], received.at[gy, 0:5], own_sem)
    keep.start()
    for copy in near + rims + far:
        copy.wait_send()
    keep.wait()

    others = pl.ds(0, NGY - 1)
    exchange(outgoing.at[others, 0:5], received.at[others, 0:5], gy).wait()

    low_level, high_level = DEPTH * gz, DEPTH * gz + 1
    arrived = received.reshape(NGY * 8, 128)
    exponent = arrived[pl.ds(4, NGY, stride=8), :]
    scale = jnp.exp2(exponent.astype(F32) * (1.0 / 64.0)) * (1.0 / 32767.0)
    words = [arrived[pl.ds(c, NGY, stride=8), :] for c in range(4)]
    turned = [(((w << 16) >> 16).astype(F32) * scale).T for w in words]
    turned += [((w >> 16).astype(F32) * scale).T for w in words]
    sign = jnp.where(iota((128, 128), 1) < 64, 1.0, -1.0)
    front = iota((8, 128), 1) < 64

    def edge(d, given, kept, kind):
        there = lax.rem(gz + d, NGZ)
        return pltpu.make_async_remote_copy(
            src_ref=given.at[jnp.where(there > gz, 0, 1)],
            dst_ref=kept.at[gz],
            send_sem=edge_send.at[kind, d],
            recv_sem=edge_recv.at[kind, d],
            device_id=(there, gy),
            device_id_type=MESH,
        )

    crossing = []
    for chi in range(2):
        mine = slice(8 * chi, 8 * chi + 8)
        left = jnp.concatenate(
            [
                jnp.concatenate([t[64 * chi : 64 * chi + 32], t[64 * chi + 32 : 64 * chi + 64]], 1)
                for t in turned
            ],
            0,
        )
        high, low = split(left)
        both = dot(jnp.concatenate([high, low], 0), y_first[...])
        value = both[0:256, 0:128] + both[256:512, 0:128] + both[0:256, 128:256]
        value = value.reshape(16, 16, 128)
        swapped = pltpu.roll(value, 64, 2)
        value = (value * turn[0] + swapped * turn[1]).reshape(8, 2, 16, 128)
        right = jnp.concatenate([value[:, z].reshape(128, 128) for z in range(DEPTH)], 1)
        high, low = split(right)
        by_high = dot(y_second[...], high)
        by_low = dot(y_second[0:256], low)
        both = by_high[0:256] + by_high[256:512] + by_low
        for z in range(DEPTH):
            lanes = slice(128 * z, 128 * z + 128)
            value = both[0:128, lanes] + pltpu.roll(both[128:256, lanes], 64, 1) * sign
            for pair in range(8):
                one, two = value[16 * pair : 16 * pair + 8], value[16 * pair + 8 : 16 * pair + 16]
                where = slice(128 * ((pair + 4) % 8), 128 * ((pair + 4) % 8) + 128)
                kept = inside[mine, where]
                spectrum[0, z, mine, where] = jnp.where(front, one, pltpu.roll(two, 64, 1)) * kept
                spectrum[1, z, mine, where] = jnp.where(front, pltpu.roll(one, 64, 1), two) * kept

        up = below[high_level] * pivots[2, low_level, mine]
        down = above[low_level] * pivots[3, high_level, mine]
        for side in range(2):
            near_level, far_level, weight = (1, 0, up) if side == 0 else (0, 1, down)
            values = [
                spectrum[part, near_level, mine] - weight * spectrum[part, far_level, mine]
                for part in range(2)
            ]
            largest = jnp.maximum(jnp.abs(values[0]), jnp.abs(values[1]))
            largest = jnp.maximum(jnp.max(largest, axis=1, keepdims=True), 1e-30)
            scale = 32767.0 / largest
            codes = jnp.concatenate([jnp.floor(v * scale + 0.5).astype(I32) for v in values], 0)
            edges[chi, side] = codes.astype(jnp.int16)
            steps[chi, side] = jnp.broadcast_to(largest * (1.0 / 32767.0), (8, 128))
        copies = [
            edge(d, given.at[chi], kept.at[chi], 2 * chi + kind)
            for d in (2, 1, 3)
            for kind, (given, kept) in enumerate(((edges, edge_in), (steps, steps_in)))
        ]
        for copy in copies:
            copy.start()
        edge_in[chi, gz] = jnp.zeros((16, NY), jnp.int16)
        steps_in[chi, gz] = jnp.zeros((8, 128), F32)
        crossing.append(copies)

    beneath = jnp.maximum(low_level - 1, 0)
    over = jnp.minimum(high_level + 1, NZ - 1)
    cross_up, cross_down = below[high_level], above[low_level]
    for chi in range(2):
        mine = slice(8 * chi, 8 * chi + 8)
        first_pivot, last_pivot = pivots[0, low_level, mine], pivots[1, high_level, mine]
        inverse = 1.0 / (first_pivot * last_pivot - cross_up * cross_down)
        from_below = below[low_level] * pivots[2, beneath, mine]
        from_above = above[high_level] * pivots[3, over, mine]
        for copy in crossing[chi]:
            copy.wait()

        def edges_of(block):
            step = jnp.concatenate([steps_in[chi, block]] * (NY // 128), 1)
            codes = edge_in[chi, block].astype(I32).astype(F32)
            return codes[0:8] * step, codes[8:16] * step

        arriving = [edges_of(block) for block in range(NGZ)]
        for part in range(2):
            reached = jnp.zeros((8, NY), F32)
            for block in range(NGZ - 1):
                new = arriving[block][part]
                if block > 0:
                    k = DEPTH * block
                    along = pivots[2, k - 1, mine] * pivots[2, k, mine]
                    new = new + (below[k] * below[k + 1]) * along * reached
                reached = jnp.where(block < gz, new, reached)
            lower = spectrum[part, 0, mine] - from_below * reached
            reached = jnp.zeros((8, NY), F32)
            for block in range(NGZ - 1, 0, -1):
                new = arriving[block][part]
                if block < NGZ - 1:
                    k = DEPTH * block
                    along = pivots[3, k + 1, mine] * pivots[3, k + 2, mine]
                    new = new + (above[k] * above[k + 1]) * along * reached
                reached = jnp.where(block > gz, new, reached)
            upper = spectrum[part, 1, mine] - from_above * reached
            for z, value in enumerate(
                (last_pivot * lower - cross_down * upper, first_pivot * upper - cross_up * lower)
            ):
                value = value * inverse
                for tile in range(NY // 128):
                    out[pl.ds(256 * chi + part * 16 + tile * 2 + z, 8, stride=32), :] = value[
                        :, tile * 128 : (tile + 1) * 128
                    ]


def per_device(velocity_x, velocity_y, velocity_z, owners, below, above, metric):
    anywhere = pl.BlockSpec(memory_space=pl.ANY)
    scalars = pl.BlockSpec(memory_space=pltpu.SMEM)
    consts = [jnp.asarray(t) for t in tables()]
    dma = pltpu.SemaphoreType.DMA
    result = pl.pallas_call(
        kernel,
        out_shape=pltpu.VMEM((2 * DEPTH * CAP * NY // 128, 128), F32),
        in_specs=[anywhere] * 4 + [scalars] * 3 + [anywhere] * 5,
        out_specs=pl.BlockSpec(memory_space=pltpu.VMEM),
        scratch_shapes=[
            pltpu.VMEM((3, DEPTH, ROWS, NX), BF16),
            pltpu.VMEM((1, KXR), I32),
            pltpu.VMEM((3 * DEPTH * ROWS * 16, 128), F32),
            pltpu.VMEM((3, 6, 20, 16, 128), BF16),
            pltpu.VMEM((6, 4, 18, 16, 128), F32),
            pltpu.VMEM((3, 2, 18, 16, 128), F32),
            pltpu.VMEM((DEPTH, ROWS, 16, 128), F32),
            pltpu.VMEM((2, 256, 256), BF16),
            pltpu.VMEM((NGY, 8, 128), I32),
            pltpu.VMEM((NGY, 8, 128), I32),
        ]
        + [pltpu.VMEM(c.shape, c.dtype) for c in consts]
        + [
            pltpu.VMEM((4, 256, KXR), BF16),
            pltpu.VMEM((4, NZ, CAP, NY), F32),
            pltpu.VMEM((2, 2, 16, NY), jnp.int16),
            pltpu.VMEM((2, NGZ, 16, NY), jnp.int16),
            pltpu.VMEM((2, 2, 8, 128), F32),
            pltpu.VMEM((2, NGZ, 8, 128), F32),
            pltpu.VMEM((2, DEPTH, CAP, NY), F32),
            dma((9,)), dma((14,)), dma((14,)), dma(()), dma(()), dma((4, NGZ)), dma((4, NGZ)),
            dma(()),
            pltpu.SemaphoreType.REGULAR((5,)),
        ],
        compiler_params=pltpu.CompilerParams(collective_id=0, has_side_effects=True),
    )(velocity_x, velocity_y, velocity_z, owners.reshape(1, KXR), below, above, metric, *consts)
    result = result.reshape(CAP, 2, NY // 128, DEPTH, 128)
    return jnp.transpose(result, (0, 1, 3, 2, 4)).reshape(1, CAP, 2, DEPTH, NY)


def solution(mesh):
    placed = (P("gz", "gy", None), P("gz", "gy", None), P("gz", "gy", None), P(), P(), P(), P())
    return jax.shard_map(
        per_device,
        mesh=mesh,
        in_specs=placed,
        out_specs=P("gy", None, None, "gz", None),
        check_vma=False,
    )
```

```python
import functools
import math

import jax
import jax.numpy as jnp
import ml_dtypes
import numpy as np
from jax import lax
from jax.experimental import pallas as pl
from jax.experimental.pallas import tpu as pltpu
from jax.sharding import PartitionSpec as P

MESH = pl.DeviceIdType.MESH
F32, BF16, I32 = jnp.float32, jnp.bfloat16, jnp.int32
SMAG_COEF = 0.12
STRAIN_FLOOR = 0.01
BASE_SHIFT = 0.004
MODE_SHIFT = 0.02
NX, NY, NZ, KXR, CAP = 2048, 1024, 8, 512, 16
NGZ, NGY = 4, 64
DEPTH, ROWS = 2, 16
STRAIGHT = ((1, 0), (-1, 0), (0, 1), (0, -1))


def halves(table):
    high = table.astype(ml_dtypes.bfloat16)
    low = (table - high.astype(np.float64)).astype(ml_dtypes.bfloat16)
    return high, low


def tables():
    a = np.arange(16)
    first = np.zeros((16, 16))
    first[0], first[1] = 1.0, (-1.0) ** a
    for r in range(1, 8):
        first[2 * r] = np.cos(2 * np.pi * ((r * a) % 16) / 16)
        first[2 * r + 1] = -np.sin(2 * np.pi * ((r * a) % 16) / 16)
    spread = np.einsum("ca,rs->crsa", first, np.eye(16)).reshape(256, 256)
    x_first = np.stack(halves(spread))

    b = np.arange(128)
    q = np.arange(32)
    second = np.zeros((8, 2, 128, 2, 2, 32))
    for i in range(8):
        for which, r in enumerate((i, 8 if i == 0 else 16 - i)):
            angle = 2 * np.pi * ((b[:, None] * (16 * q[None, :] + r)) % NX) / NX
            c, s = np.cos(angle), np.sin(angle)
            if i == 0:
                second[i, which, :, 0, which] = c
                second[i, which, :, 1, which] = -s
            else:
                sign = 1.0 if which == 0 else -1.0
                second[i, 0, :, 0, which] = c
                second[i, 1, :, 0, which] = sign * s
                second[i, 0, :, 1, which] = -s
                second[i, 1, :, 1, which] = sign * c
    second = second.reshape(8, 256, 128) / math.sqrt(NX * NY)
    x_second = np.concatenate(halves(second), axis=2)

    s64 = np.arange(64)
    angle = 2 * np.pi * ((s64[:, None] * s64[None, :]) % 64) / 64
    c, s = np.cos(angle), np.sin(angle)
    y_first = np.concatenate([np.concatenate([c, -s], 1), np.concatenate([s, c], 1)], 0)
    y_first = np.concatenate(halves(y_first), axis=1)

    j = np.arange(16)
    angle = 2 * np.pi * (j[:, None] * s64[None, :]) / NY
    c, s = np.cos(angle), np.sin(angle)
    turn = np.stack([np.concatenate([c, c], 1), np.concatenate([s, -s], 1)]).astype(np.float32)

    angle = 2 * np.pi * ((j[:, None] * j[None, :]) % 16) / 16
    both = np.stack([np.cos(angle), np.sin(angle)])
    spread = np.einsum("pqj,yv->pqyvj", both, np.eye(8)).reshape(256, 128)
    y_second = np.concatenate(halves(spread), axis=0)
    return x_first, x_second, y_first, turn, y_second


def split(value):
    high = value.astype(BF16)
    return high, (value - high.astype(F32)).astype(BF16)


def dot(left, right):
    return jnp.dot(left, right, preferred_element_type=F32)


def mode_of(position):
    block, which, q = position // 64, (position // 32) % 2, position % 32
    r = jnp.where(which == 0, block, jnp.where(block == 0, 8, 16 - block))
    return 16 * q + r


def iota(shape, dim):
    return lax.broadcasted_iota(I32, shape, dim)


def next_x(field, ahead):
    if ahead:
        turned = pltpu.roll(field, 127, 2)
        return jnp.where(iota(field.shape, 2) == 127, pltpu.roll(turned, 15, 1), turned)
    turned = pltpu.roll(field, 1, 2)
    return jnp.where(iota(field.shape, 2) == 0, pltpu.roll(turned, 1, 1), turned)


def kernel(
    vx, vy, vz, owners_in, below, above, metric, x_first_in, x_second_in, y_first_in, turn_in,
    y_second_in, out,
    own, owners, spread, ext, stress, flat, begun, source, outgoing, received, x_first, x_second, y_first, turn,
    y_second, chosen, pivots, edges, edge_in, steps, steps_in, spectrum,
    in_sem, halo_send, halo_recv, all_send, all_recv, edge_send, edge_recv, own_sem, meeting,
):
    gz, gy = lax.axis_index("gz"), lax.axis_index("gy")

    def peer(dz, dy):
        return (lax.rem(gz + dz + NGZ, NGZ), lax.rem(gy + dy + NGY, NGY))

    loads = [pltpu.make_async_copy(v, own.at[i], in_sem.at[i]) for i, v in enumerate((vx, vy, vz))]
    for index, (given, kept) in enumerate(
        ((owners_in, owners), (x_first_in, x_first), (x_second_in, x_second), (y_first_in, y_first), (turn_in, turn),
         (y_second_in, y_second))
    ):
        loads.append(pltpu.make_async_copy(given, kept, in_sem.at[3 + index]))
    for load in loads:
        load.start()

    barrier = pltpu.get_barrier_semaphore()

    for dz, dy in STRAIGHT:
        pl.semaphore_signal(barrier, inc=1, device_id=peer(dz, dy), device_id_type=MESH)

    for c in range(3):
        loads[c].wait()
    for c in range(3):
        for z in range(DEPTH):
            base = (c * DEPTH + z) * ROWS * 16
            for a in range(16):
                spread[pl.ds(base + a, 16, stride=16), :] = own[
                    c, z, :, a * 128 : (a + 1) * 128
                ].astype(F32)
            ext[c, z + 2, 2:18] = spread[base : base + 256, :].reshape(16, 16, 128).astype(BF16)

    pl.semaphore_wait(barrier, len(STRAIGHT))

    def copy_to(index, dz, dy, given, kept):
        return pltpu.make_async_remote_copy(
            src_ref=ext.at[:, given[0], given[1]],
            dst_ref=ext.at[:, kept[0], kept[1]],
            send_sem=halo_send.at[index],
            recv_sem=halo_recv.at[index],
            device_id=peer(dz, dy),
            device_id_type=MESH,
        )

    def rows(start, count):
        return pl.ds(start, count)

    near = [
        copy_to(0, 1, 0, (pl.ds(3, 1), rows(2, 16)), (pl.ds(1, 1), rows(2, 16))),
        copy_to(1, -1, 0, (pl.ds(2, 1), rows(2, 16)), (pl.ds(4, 1), rows(2, 16))),
    ]
    rims = [
        copy_to(2, 0, 1, (pl.ds(2, 2), rows(16, 2)), (pl.ds(2, 2), rows(0, 2))),
        copy_to(3, 0, -1, (pl.ds(2, 2), rows(2, 2)), (pl.ds(2, 2), rows(18, 2))),
    ]
    far = [
        copy_to(4, 1, 1, (pl.ds(2, 1), rows(17, 1)), (pl.ds(0, 1), rows(1, 1))),
        copy_to(5, 1, -1, (pl.ds(2, 1), rows(2, 1)), (pl.ds(0, 1), rows(18, 1))),
        copy_to(6, -1, 1, (pl.ds(3, 1), rows(17, 1)), (pl.ds(5, 1), rows(1, 1))),
        copy_to(7, -1, -1, (pl.ds(3, 1), rows(2, 1)), (pl.ds(5, 1), rows(18, 1))),
        copy_to(8, 1, 0, (pl.ds(2, 1), rows(2, 16)), (pl.ds(0, 1), rows(2, 16))),
        copy_to(9, -1, 0, (pl.ds(3, 1), rows(2, 16)), (pl.ds(5, 1), rows(2, 16))),
    ]
    corners = [
        copy_to(10, 0, 1, (pl.ds(1, 1), rows(16, 2)), (pl.ds(1, 1), rows(0, 2))),
        copy_to(11, 0, 1, (pl.ds(4, 1), rows(16, 2)), (pl.ds(4, 1), rows(0, 2))),
        copy_to(12, 0, -1, (pl.ds(1, 1), rows(2, 2)), (pl.ds(1, 1), rows(18, 2))),
        copy_to(13, 0, -1, (pl.ds(4, 1), rows(2, 2)), (pl.ds(4, 1), rows(18, 2))),
    ]
    for copy in near + rims:
        copy.start()

    def meet(number, peers):
        for dz, dy in peers:
            pl.semaphore_signal(meeting.at[number], inc=1, device_id=peer(dz, dy), device_id_type=MESH)

    meet(0, STRAIGHT)
    pl.semaphore_wait(meeting.at[0], len(STRAIGHT))
    for copy in far:
        copy.start()
    meet(1, ((0, 2), (0, -2)))

    loads[3].wait()
    owner_row = owners[...]
    kx_row = mode_of(iota((1, KXR), 1))
    named = jnp.where(owner_row == iota((NGY, KXR), 0), 1.0, 0.0).astype(BF16)
    place = jnp.where(iota((KXR, KXR), 0) == kx_row, 1.0, 0.0).astype(BF16)
    named = dot(named, place)
    smaller = jnp.where(mode_of(iota((KXR, 1), 0)) < kx_row, 1.0, 0.0).astype(BF16)
    rank = dot(named.astype(BF16), smaller)
    slot_row = jnp.sum(
        named * (rank + CAP * iota((NGY, KXR), 0).astype(F32)), axis=0, keepdims=True
    ).astype(I32)
    for k in range(4):
        m = iota((256, 1), 0)
        slot_id = (m // 4) * CAP + k * 4 + m % 4
        chosen[k] = jnp.where(slot_row == slot_id, 1.0, 0.0).astype(BF16)
    mine = slot_row == gy * CAP + iota((CAP, KXR), 0)
    own_kx = jnp.sum(jnp.where(mine, kx_row.astype(F32), 0.0), axis=1, keepdims=True)
    own_ok = jnp.sum(jnp.where(mine, 1.0, 0.0), axis=1, keepdims=True)
    ky = (iota((1, NY), 1) - KXR).astype(F32)
    radius = own_kx * own_kx + ky * ky
    inside = jnp.where(radius <= float(KXR * KXR), 1.0, 0.0) * own_ok


    shift = BASE_SHIFT + MODE_SHIFT * (radius / float(KXR * KXR))
    for k in range(NZ):
        pivot = -(below[k] + above[k] + metric[k] * shift)
        if k > 0:
            pivot = pivot - below[k] * above[k - 1] * pivots[2, k - 1]
        pivots[0, k] = pivot
        pivots[2, k] = 1.0 / pivot
    for k in range(NZ - 1, -1, -1):
        pivot = -(below[k] + above[k] + metric[k] * shift)
        if k < NZ - 1:
            pivot = pivot - above[k] * below[k + 1] * pivots[3, k + 1]
        pivots[1, k] = pivot
        pivots[3, k] = 1.0 / pivot

    pl.semaphore_wait(meeting.at[1], 2)
    meet(2, ((0, 4), (0, -4)))

    def zero_rim(levels):
        @pl.when(gy == 0)
        def _():
            for level in levels:
                ext[:, level, 0:2] = jnp.zeros((3, 2, 16, 128), BF16)

        @pl.when(gy == NGY - 1)
        def _():
            for level in levels:
                ext[:, level, 18:20] = jnp.zeros((3, 2, 16, 128), BF16)

    def zero_level(edge, level, start, count):
        @pl.when(gz == edge)
        def _():
            for c in range(3):
                ext[c, level, start : start + count] = jnp.zeros((count, 16, 128), BF16)

    def at(c, level, row, count):
        return ext[c, level, pl.ds(row, count)].astype(F32)

    def flat_slopes(level, row, count):
        centre = [at(c, level, row, count) for c in range(3)]
        dx = [(next_x(f, True) - next_x(f, False)) * 0.5 for f in centre]
        dy = [(at(c, level, row + 1, count) - at(c, level, row - 1, count)) * 0.5 for c in range(3)]
        return dx, dy

    def slopes_z(level, row, count):
        return [(at(c, level + 1, row, count) - at(c, level - 1, row, count)) * 0.5 for c in range(3)]

    near[0].wait_recv()
    zero_level(0, 1, 2, 16)
    corners[0].start()
    corners[2].start()
    near[1].wait_recv()
    zero_level(NGZ - 1, 4, 2, 16)
    corners[1].start()
    corners[3].start()
    for copy in rims + corners:
        copy.wait_recv()
    for copy in corners:
        copy.wait_send()
    zero_level(0, 1, 0, 20)
    zero_level(NGZ - 1, 4, 0, 20)
    zero_rim((1, 2, 3, 4))

    @pl.loop(0, 18, unroll=6)
    def _(step):
        level, row, count = 2 + step // 9, 1 + 2 * lax.rem(step, 9), 2
        dx, dy = flat_slopes(level, row, count)
        grad = list(zip(dx, dy, slopes_z(level, row, count)))
        strain = {
            (i, j): grad[i][i] if i == j else 0.5 * (grad[i][j] + grad[j][i])
            for i in range(3) for j in range(i, 3)
        }
        squared = 2.0 * sum(strain[i, i] * strain[i, i] for i in range(3))
        squared = squared + 4.0 * sum(
            strain[i, j] * strain[i, j] for i in range(3) for j in range(i + 1, 3)
        )
        viscous = 2.0 * SMAG_COEF * jnp.sqrt(squared + STRAIN_FLOOR)
        for index, pair in enumerate(((2, 2), (0, 2), (1, 2), (0, 0), (0, 1), (1, 1))):
            stress[index, level - 1, pl.ds(row - 1, count)] = viscous * strain[pair]

    pl.semaphore_wait(meeting.at[2], 2)
    meet(3, ((0, 8), (0, -8)))

    @pl.loop(0, 18, unroll=6)
    def _(step):
        side, row, count = step // 9, 1 + 2 * lax.rem(step, 9), 2
        dx, dy = flat_slopes(1 + 3 * side, row, count)
        mixed = 0.5 * (dy[0] + dx[1])
        squared = 2.0 * (dx[0] * dx[0] + dy[1] * dy[1]) + 4.0 * mixed * mixed + STRAIN_FLOOR
        for index, value in enumerate((squared, dx[2], dy[2])):
            flat[index, side, pl.ds(row - 1, count)] = value

    for z in range(DEPTH):

        @pl.loop(0, 8, unroll=8)
        def _(step):
            row = 2 * step
            sign = 1.0 if z == 0 else -1.0

            def part(index, dz, dy):
                return stress[index, z + 1 + dz, pl.ds(row + 1 + dy, 2)]

            def wind(c, dz, dy):
                return at(c, z + 2 + dz, row + 2 + dy, 2)

            beside = 1 - 2 * z
            total = 0.5 * (wind(1, 0, 1) - wind(1, 0, -1) + wind(2, 1, 0) - wind(2, -1, 0))
            total = total + part(5, 0, 1) + part(5, 0, -1) + part(0, beside, 0)
            total = total - 2.0 * (part(3, 0, 0) + part(5, 0, 0) + part(0, 0, 0))
            total = total + (0.5 * sign) * (part(2, beside, 1) - part(2, beside, -1))
            odd = 0.5 * (wind(0, 0, 0) + part(4, 0, 1) - part(4, 0, -1) + sign * part(1, beside, 0))
            even = part(3, 0, 0)
            total = total + next_x(even + odd, True) + next_x(even - odd, False)
            begun[z, pl.ds(row, 2)] = total

    pl.semaphore_wait(meeting.at[3], 2)
    meet(4, ((0, 16), (0, -16)))

    for copy in far:
        copy.wait_recv()
    zero_level(0, 0, 0, 20)
    zero_level(NGZ - 1, 5, 0, 20)
    zero_rim((0, 5))

    @pl.loop(0, 18, unroll=6)
    def _(step):
        side, row, count = step // 9, 1 + 2 * lax.rem(step, 9), 2
        level = 1 + 3 * side
        dz = slopes_z(level, row, count)
        squared, dx_w, dy_w = (flat[index, side, pl.ds(row - 1, count)] for index in range(3))
        strain_x, strain_y = 0.5 * (dz[0] + dx_w), 0.5 * (dz[1] + dy_w)
        squared = squared + 2.0 * dz[2] * dz[2] + 4.0 * (strain_x * strain_x + strain_y * strain_y)
        viscous = 2.0 * SMAG_COEF * jnp.sqrt(squared)
        for index, value in enumerate((dz[2], strain_x, strain_y)):
            stress[index, level - 1, pl.ds(row - 1, count)] = viscous * value

    for z in range(DEPTH):

        @pl.loop(0, 8, unroll=8)
        def _(step):
            row = 2 * step
            sign = -1.0 if z == 0 else 1.0

            def part(index, dy):
                return stress[index, 3 * z, pl.ds(row + 1 + dy, 2)]

            odd = (0.5 * sign) * part(1, 0)
            total = begun[z, pl.ds(row, 2)] + part(0, 0)
            total = total + (0.5 * sign) * (part(2, 1) - part(2, -1))
            total = total + next_x(odd, True) - next_x(odd, False)
            high, low = split(total.reshape(32, 128))
            start = pl.multiple_of(32 * step, 32)
            source[0, pl.ds(start, 32), z * 128 : (z + 1) * 128] = high
            source[1, pl.ds(start, 32), z * 128 : (z + 1) * 128] = low

    for load in loads[4:]:
        load.wait()
    high, low = source[0], source[1]
    first = dot(x_first[0], high) + dot(x_first[0], low) + dot(x_first[1], high)
    parts = []
    for i in range(8):
        lines = first[32 * i : 32 * i + 32]
        left = jnp.concatenate(
            [
                jnp.concatenate(
                    [lines[0:16, 128 * z : 128 * z + 128], lines[16:32, 128 * z : 128 * z + 128]], 1
                )
                for z in range(DEPTH)
            ],
            0,
        )
        high, low = split(left)
        both = dot(jnp.concatenate([high, low], 0), x_second[i])
        value = both[0:32, 0:128] + both[32:64, 0:128] + both[0:32, 128:256]
        parts.append(value)
    pieces = []
    for i in range(0, 8, 2):
        one, two = parts[i], parts[i + 1]
        front = iota((32, 128), 1) < 64
        real = jnp.where(front, one, pltpu.roll(two, 64, 1))
        imag = jnp.where(front, pltpu.roll(one, 64, 1), two)
        pieces.append(jnp.concatenate([real, imag], 0))
    modes = jnp.concatenate(pieces, 1)
    high, low = split(modes)
    modes = jnp.concatenate([high, low], 0)
    slots = []
    for k in range(4):
        taken = lax.dot_general(
            chosen[k], modes, (((1,), (1,)), ((), ())), preferred_element_type=F32
        )
        slots.append(taken + pltpu.roll(taken, 64, 1))
    front = iota((256, 128), 1) < 64
    low, high = jnp.where(front, slots[0], slots[2]), jnp.where(front, slots[1], slots[3])
    largest = jnp.max(jnp.maximum(jnp.abs(low), jnp.abs(high)), axis=0, keepdims=True)
    exponent = jnp.ceil(jnp.log2(jnp.maximum(largest, 1e-30)) * 64.0) + 1.0
    scale = 32767.0 * jnp.exp2(exponent * (-1.0 / 64.0))
    low, high = (jnp.floor(v * scale + 0.5).astype(I32) for v in (low, high))
    words = (high << 16) | (low & 0xFFFF)
    for g in range(NGY):
        outgoing[g, 0:4] = words[4 * g : 4 * g + 4]
    outgoing[:, 4:5] = jnp.broadcast_to(exponent.astype(I32)[None], (NGY, 1, 128))

    pl.semaphore_wait(meeting.at[4], 2)

    def exchange(given, kept, there):
        return pltpu.make_async_remote_copy(
            src_ref=given,
            dst_ref=kept,
            send_sem=all_send,
            recv_sem=all_recv,
            device_id=(gz, there),
            device_id_type=MESH,
        )

    def away(half, k):
        return half + (k + 1) // 2 * (1 - 2 * lax.rem(k, 2))

    @pl.loop(0, NGY - 1, unroll=3)
    def _(k):
        step_z, step_y = away(4, lax.rem(k // 2, 8)), away(2, k // 16)
        there = (
            lax.rem(gy // 8 + step_z, 8) * 8
            + lax.rem(lax.rem(gy // 2, 4) + step_y, 4) * 2
            + lax.rem(gy + 1 + k, 2)
        )
        exchange(outgoing.at[there, 0:5], received.at[gy, 0:5], there).start()

    keep = pltpu.make_async_copy(outgoing.at[gy, 0:5], received.at[gy, 0:5], own_sem)
    keep.start()
    for copy in near + rims + far:
        copy.wait_send()
    keep.wait()

    others = pl.ds(0, NGY - 1)
    exchange(outgoing.at[others, 0:5], received.at[others, 0:5], gy).wait()

    low_level, high_level = DEPTH * gz, DEPTH * gz + 1
    arrived = received.reshape(NGY * 8, 128)
    exponent = arrived[pl.ds(4, NGY, stride=8), :]
    scale = jnp.exp2(exponent.astype(F32) * (1.0 / 64.0)) * (1.0 / 32767.0)
    words = [arrived[pl.ds(c, NGY, stride=8), :] for c in range(4)]
    turned = [(((w << 16) >> 16).astype(F32) * scale).T for w in words]
    turned += [((w >> 16).astype(F32) * scale).T for w in words]
    sign = jnp.where(iota((128, 128), 1) < 64, 1.0, -1.0)
    front = iota((8, 128), 1) < 64

    def edge(d, given, kept, kind):
        there = lax.rem(gz + d, NGZ)
        return pltpu.make_async_remote_copy(
            src_ref=given.at[jnp.where(there > gz, 0, 1)],
            dst_ref=kept.at[gz],
            send_sem=edge_send.at[kind, d],
            recv_sem=edge_recv.at[kind, d],
            device_id=(there, gy),
            device_id_type=MESH,
        )

    crossing = []
    for chi in range(2):
        mine = slice(8 * chi, 8 * chi + 8)
        left = jnp.concatenate(
            [
                jnp.concatenate([t[64 * chi : 64 * chi + 32], t[64 * chi + 32 : 64 * chi + 64]], 1)
                for t in turned
            ],
            0,
        )
        high, low = split(left)
        both = dot(jnp.concatenate([high, low], 0), y_first[...])
        value = both[0:256, 0:128] + both[256:512, 0:128] + both[0:256, 128:256]
        value = value.reshape(16, 16, 128)
        swapped = pltpu.roll(value, 64, 2)
        value = (value * turn[0] + swapped * turn[1]).reshape(8, 2, 16, 128)
        right = jnp.concatenate([value[:, z].reshape(128, 128) for z in range(DEPTH)], 1)
        high, low = split(right)
        by_high = dot(y_second[...], high)
        by_low = dot(y_second[0:256], low)
        both = by_high[0:256] + by_high[256:512] + by_low
        for z in range(DEPTH):
            lanes = slice(128 * z, 128 * z + 128)
            value = both[0:128, lanes] + pltpu.roll(both[128:256, lanes], 64, 1) * sign
            for pair in range(8):
                one, two = value[16 * pair : 16 * pair + 8], value[16 * pair + 8 : 16 * pair + 16]
                where = slice(128 * ((pair + 4) % 8), 128 * ((pair + 4) % 8) + 128)
                kept = inside[mine, where]
                spectrum[0, z, mine, where] = jnp.where(front, one, pltpu.roll(two, 64, 1)) * kept
                spectrum[1, z, mine, where] = jnp.where(front, pltpu.roll(one, 64, 1), two) * kept

        up = below[high_level] * pivots[2, low_level, mine]
        down = above[low_level] * pivots[3, high_level, mine]
        for side in range(2):
            near_level, far_level, weight = (1, 0, up) if side == 0 else (0, 1, down)
            values = [
                spectrum[part, near_level, mine] - weight * spectrum[part, far_level, mine]
                for part in range(2)
            ]
            largest = jnp.maximum(jnp.abs(values[0]), jnp.abs(values[1]))
            largest = jnp.maximum(jnp.max(largest, axis=1, keepdims=True), 1e-30)
            scale = 32767.0 / largest
            codes = jnp.concatenate([jnp.floor(v * scale + 0.5).astype(I32) for v in values], 0)
            edges[chi, side] = codes.astype(jnp.int16)
            steps[chi, side] = jnp.broadcast_to(largest * (1.0 / 32767.0), (8, 128))
        copies = [
            edge(d, given.at[chi], kept.at[chi], 2 * chi + kind)
            for d in (1, 3, 2)
            for kind, (given, kept) in enumerate(((edges, edge_in), (steps, steps_in)))
        ]
        for copy in copies:
            copy.start()
        edge_in[chi, gz] = jnp.zeros((16, NY), jnp.int16)
        steps_in[chi, gz] = jnp.zeros((8, 128), F32)
        crossing.append(copies)

    beneath = jnp.maximum(low_level - 1, 0)
    over = jnp.minimum(high_level + 1, NZ - 1)
    cross_up, cross_down = below[high_level], above[low_level]
    for chi in range(2):
        mine = slice(8 * chi, 8 * chi + 8)
        first_pivot, last_pivot = pivots[0, low_level, mine], pivots[1, high_level, mine]
        inverse = 1.0 / (first_pivot * last_pivot - cross_up * cross_down)
        from_below = below[low_level] * pivots[2, beneath, mine]
        from_above = above[high_level] * pivots[3, over, mine]
        for copy in crossing[chi]:
            copy.wait()

        def edges_of(block):
            step = jnp.concatenate([steps_in[chi, block]] * (NY // 128), 1)
            codes = edge_in[chi, block].astype(I32).astype(F32)
            return codes[0:8] * step, codes[8:16] * step

        arriving = [edges_of(block) for block in range(NGZ)]
        for part in range(2):
            reached = jnp.zeros((8, NY), F32)
            for block in range(NGZ - 1):
                new = arriving[block][part]
                if block > 0:
                    k = DEPTH * block
                    along = pivots[2, k - 1, mine] * pivots[2, k, mine]
                    new = new + (below[k] * below[k + 1]) * along * reached
                reached = jnp.where(block < gz, new, reached)
            lower = spectrum[part, 0, mine] - from_below * reached
            reached = jnp.zeros((8, NY), F32)
            for block in range(NGZ - 1, 0, -1):
                new = arriving[block][part]
                if block < NGZ - 1:
                    k = DEPTH * block
                    along = pivots[3, k + 1, mine] * pivots[3, k + 2, mine]
                    new = new + (above[k] * above[k + 1]) * along * reached
                reached = jnp.where(block > gz, new, reached)
            upper = spectrum[part, 1, mine] - from_above * reached
            for z, value in enumerate(
                (last_pivot * lower - cross_down * upper, first_pivot * upper - cross_up * lower)
            ):
                value = value * inverse
                for tile in range(NY // 128):
                    out[pl.ds(256 * chi + part * 16 + tile * 2 + z, 8, stride=32), :] = value[
                        :, tile * 128 : (tile + 1) * 128
                    ]


def per_device(velocity_x, velocity_y, velocity_z, owners, below, above, metric):
    anywhere = pl.BlockSpec(memory_space=pl.ANY)
    scalars = pl.BlockSpec(memory_space=pltpu.SMEM)
    consts = [jnp.asarray(t) for t in tables()]
    dma = pltpu.SemaphoreType.DMA
    result = pl.pallas_call(
        kernel,
        out_shape=pltpu.VMEM((2 * DEPTH * CAP * NY // 128, 128), F32),
        in_specs=[anywhere] * 4 + [scalars] * 3 + [anywhere] * 5,
        out_specs=pl.BlockSpec(memory_space=pltpu.VMEM),
        scratch_shapes=[
            pltpu.VMEM((3, DEPTH, ROWS, NX), BF16),
            pltpu.VMEM((1, KXR), I32),
            pltpu.VMEM((3 * DEPTH * ROWS * 16, 128), F32),
            pltpu.VMEM((3, 6, 20, 16, 128), BF16),
            pltpu.VMEM((6, 4, 18, 16, 128), F32),
            pltpu.VMEM((3, 2, 18, 16, 128), F32),
            pltpu.VMEM((DEPTH, ROWS, 16, 128), F32),
            pltpu.VMEM((2, 256, 256), BF16),
            pltpu.VMEM((NGY, 8, 128), I32),
            pltpu.VMEM((NGY, 8, 128), I32),
        ]
        + [pltpu.VMEM(c.shape, c.dtype) for c in consts]
        + [
            pltpu.VMEM((4, 256, KXR), BF16),
            pltpu.VMEM((4, NZ, CAP, NY), F32),
            pltpu.VMEM((2, 2, 16, NY), jnp.int16),
            pltpu.VMEM((2, NGZ, 16, NY), jnp.int16),
            pltpu.VMEM((2, 2, 8, 128), F32),
            pltpu.VMEM((2, NGZ, 8, 128), F32),
            pltpu.VMEM((2, DEPTH, CAP, NY), F32),
            dma((9,)), dma((14,)), dma((14,)), dma(()), dma(()), dma((4, NGZ)), dma((4, NGZ)),
            dma(()),
            pltpu.SemaphoreType.REGULAR((5,)),
        ],
        compiler_params=pltpu.CompilerParams(collective_id=0, has_side_effects=True),
    )(velocity_x, velocity_y, velocity_z, owners.reshape(1, KXR), below, above, metric, *consts)
    result = result.reshape(CAP, 2, NY // 128, DEPTH, 128)
    return jnp.transpose(result, (0, 1, 3, 2, 4)).reshape(1, CAP, 2, DEPTH, NY)


def solution(mesh):
    placed = (P("gz", "gy", None), P("gz", "gy", None), P("gz", "gy", None), P(), P(), P(), P())
    return jax.shard_map(
        per_device,
        mesh=mesh,
        in_specs=placed,
        out_specs=P("gy", None, None, "gz", None),
        check_vma=False,
    )
```

```python
import functools
import math

import jax
import jax.numpy as jnp
import ml_dtypes
import numpy as np
from jax import lax
from jax.experimental import pallas as pl
from jax.experimental.pallas import tpu as pltpu
from jax.sharding import PartitionSpec as P

MESH = pl.DeviceIdType.MESH
F32, BF16, I32 = jnp.float32, jnp.bfloat16, jnp.int32
SMAG_COEF = 0.12
STRAIN_FLOOR = 0.01
BASE_SHIFT = 0.004
MODE_SHIFT = 0.02
NX, NY, NZ, KXR, CAP = 2048, 1024, 8, 512, 16
NGZ, NGY = 4, 64
DEPTH, ROWS = 2, 16
STRAIGHT = ((1, 0), (-1, 0), (0, 1), (0, -1))


def halves(table):
    high = table.astype(ml_dtypes.bfloat16)
    low = (table - high.astype(np.float64)).astype(ml_dtypes.bfloat16)
    return high, low


def tables():
    a = np.arange(16)
    first = np.zeros((16, 16))
    first[0], first[1] = 1.0, (-1.0) ** a
    for r in range(1, 8):
        first[2 * r] = np.cos(2 * np.pi * ((r * a) % 16) / 16)
        first[2 * r + 1] = -np.sin(2 * np.pi * ((r * a) % 16) / 16)
    spread = np.einsum("ca,rs->crsa", first, np.eye(16)).reshape(256, 256)
    x_first = np.stack(halves(spread))

    b = np.arange(128)
    q = np.arange(32)
    second = np.zeros((8, 2, 128, 2, 2, 32))
    for i in range(8):
        for which, r in enumerate((i, 8 if i == 0 else 16 - i)):
            angle = 2 * np.pi * ((b[:, None] * (16 * q[None, :] + r)) % NX) / NX
            c, s = np.cos(angle), np.sin(angle)
            if i == 0:
                second[i, which, :, 0, which] = c
                second[i, which, :, 1, which] = -s
            else:
                sign = 1.0 if which == 0 else -1.0
                second[i, 0, :, 0, which] = c
                second[i, 1, :, 0, which] = sign * s
                second[i, 0, :, 1, which] = -s
                second[i, 1, :, 1, which] = sign * c
    second = second.reshape(8, 256, 128) / math.sqrt(NX * NY)
    x_second = np.concatenate(halves(second), axis=2)

    s64 = np.arange(64)
    angle = 2 * np.pi * ((s64[:, None] * s64[None, :]) % 64) / 64
    c, s = np.cos(angle), np.sin(angle)
    y_first = np.concatenate([np.concatenate([c, -s], 1), np.concatenate([s, c], 1)], 0)
    y_first = np.concatenate(halves(y_first), axis=1)

    j = np.arange(16)
    angle = 2 * np.pi * (j[:, None] * s64[None, :]) / NY
    c, s = np.cos(angle), np.sin(angle)
    turn = np.stack([np.concatenate([c, c], 1), np.concatenate([s, -s], 1)]).astype(np.float32)

    angle = 2 * np.pi * ((j[:, None] * j[None, :]) % 16) / 16
    both = np.stack([np.cos(angle), np.sin(angle)])
    spread = np.einsum("pqj,yv->pqyvj", both, np.eye(8)).reshape(256, 128)
    y_second = np.concatenate(halves(spread), axis=0)
    return x_first, x_second, y_first, turn, y_second


def split(value):
    high = value.astype(BF16)
    return high, (value - high.astype(F32)).astype(BF16)


def dot(left, right):
    return jnp.dot(left, right, preferred_element_type=F32)


def mode_of(position):
    block, which, q = position // 64, (position // 32) % 2, position % 32
    r = jnp.where(which == 0, block, jnp.where(block == 0, 8, 16 - block))
    return 16 * q + r


def iota(shape, dim):
    return lax.broadcasted_iota(I32, shape, dim)


def next_x(field, ahead):
    if ahead:
        turned = pltpu.roll(field, 127, 2)
        return jnp.where(iota(field.shape, 2) == 127, pltpu.roll(turned, 15, 1), turned)
    turned = pltpu.roll(field, 1, 2)
    return jnp.where(iota(field.shape, 2) == 0, pltpu.roll(turned, 1, 1), turned)


def kernel(
    vx, vy, vz, owners_in, below, above, metric, x_first_in, x_second_in, y_first_in, turn_in,
    y_second_in, out,
    own, owners, spread, ext, stress, flat, begun, source, outgoing, received, x_first, x_second, y_first, turn,
    y_second, chosen, pivots, edges, edge_in, steps, steps_in, spectrum,
    in_sem, halo_send, halo_recv, all_send, all_recv, edge_send, edge_recv, own_sem, meeting,
):
    gz, gy = lax.axis_index("gz"), lax.axis_index("gy")

    def peer(dz, dy):
        return (lax.rem(gz + dz + NGZ, NGZ), lax.rem(gy + dy + NGY, NGY))

    barrier = pltpu.get_barrier_semaphore()

    for dz, dy in STRAIGHT:
        pl.semaphore_signal(barrier, inc=1, device_id=peer(dz, dy), device_id_type=MESH)

    loads = [pltpu.make_async_copy(v, own.at[i], in_sem.at[i]) for i, v in enumerate((vx, vy, vz))]
    for index, (given, kept) in enumerate(
        ((owners_in, owners), (x_first_in, x_first), (x_second_in, x_second), (y_first_in, y_first), (turn_in, turn),
         (y_second_in, y_second))
    ):
        loads.append(pltpu.make_async_copy(given, kept, in_sem.at[3 + index]))
    for load in loads[:4]:
        load.start()

    for c in range(3):
        loads[c].wait()
    for c in range(3):
        for z in range(DEPTH):
            base = (c * DEPTH + z) * ROWS * 16
            for a in range(16):
                spread[pl.ds(base + a, 16, stride=16), :] = own[
                    c, z, :, a * 128 : (a + 1) * 128
                ].astype(F32)
            ext[c, z + 2, 2:18] = spread[base : base + 256, :].reshape(16, 16, 128).astype(BF16)

    pl.semaphore_wait(barrier, len(STRAIGHT))

    def copy_to(index, dz, dy, given, kept):
        return pltpu.make_async_remote_copy(
            src_ref=ext.at[:, given[0], given[1]],
            dst_ref=ext.at[:, kept[0], kept[1]],
            send_sem=halo_send.at[index],
            recv_sem=halo_recv.at[index],
            device_id=peer(dz, dy),
            device_id_type=MESH,
        )

    def rows(start, count):
        return pl.ds(start, count)

    near = [
        copy_to(0, 1, 0, (pl.ds(3, 1), rows(2, 16)), (pl.ds(1, 1), rows(2, 16))),
        copy_to(1, -1, 0, (pl.ds(2, 1), rows(2, 16)), (pl.ds(4, 1), rows(2, 16))),
    ]
    rims = [
        copy_to(2, 0, 1, (pl.ds(2, 2), rows(16, 2)), (pl.ds(2, 2), rows(0, 2))),
        copy_to(3, 0, -1, (pl.ds(2, 2), rows(2, 2)), (pl.ds(2, 2), rows(18, 2))),
    ]
    far = [
        copy_to(4, 1, 1, (pl.ds(2, 1), rows(17, 1)), (pl.ds(0, 1), rows(1, 1))),
        copy_to(5, 1, -1, (pl.ds(2, 1), rows(2, 1)), (pl.ds(0, 1), rows(18, 1))),
        copy_to(6, -1, 1, (pl.ds(3, 1), rows(17, 1)), (pl.ds(5, 1), rows(1, 1))),
        copy_to(7, -1, -1, (pl.ds(3, 1), rows(2, 1)), (pl.ds(5, 1), rows(18, 1))),
        copy_to(8, 1, 0, (pl.ds(2, 1), rows(2, 16)), (pl.ds(0, 1), rows(2, 16))),
        copy_to(9, -1, 0, (pl.ds(3, 1), rows(2, 16)), (pl.ds(5, 1), rows(2, 16))),
    ]
    corners = [
        copy_to(10, 0, 1, (pl.ds(1, 1), rows(16, 2)), (pl.ds(1, 1), rows(0, 2))),
        copy_to(11, 0, 1, (pl.ds(4, 1), rows(16, 2)), (pl.ds(4, 1), rows(0, 2))),
        copy_to(12, 0, -1, (pl.ds(1, 1), rows(2, 2)), (pl.ds(1, 1), rows(18, 2))),
        copy_to(13, 0, -1, (pl.ds(4, 1), rows(2, 2)), (pl.ds(4, 1), rows(18, 2))),
    ]
    for copy in near + rims:
        copy.start()
    for load in loads[4:]:
        load.start()

    def meet(number, peers):
        for dz, dy in peers:
            pl.semaphore_signal(meeting.at[number], inc=1, device_id=peer(dz, dy), device_id_type=MESH)

    meet(0, STRAIGHT)
    pl.semaphore_wait(meeting.at[0], len(STRAIGHT))
    for copy in far:
        copy.start()
    meet(1, ((0, 2), (0, -2)))

    loads[3].wait()
    owner_row = owners[...]
    kx_row = mode_of(iota((1, KXR), 1))
    named = jnp.where(owner_row == iota((NGY, KXR), 0), 1.0, 0.0).astype(BF16)
    place = jnp.where(iota((KXR, KXR), 0) == kx_row, 1.0, 0.0).astype(BF16)
    named = dot(named, place)
    smaller = jnp.where(mode_of(iota((KXR, 1), 0)) < kx_row, 1.0, 0.0).astype(BF16)
    rank = dot(named.astype(BF16), smaller)
    slot_row = jnp.sum(
        named * (rank + CAP * iota((NGY, KXR), 0).astype(F32)), axis=0, keepdims=True
    ).astype(I32)
    for k in range(4):
        m = iota((256, 1), 0)
        slot_id = (m // 4) * CAP + k * 4 + m % 4
        chosen[k] = jnp.where(slot_row == slot_id, 1.0, 0.0).astype(BF16)
    mine = slot_row == gy * CAP + iota((CAP, KXR), 0)
    own_kx = jnp.sum(jnp.where(mine, kx_row.astype(F32), 0.0), axis=1, keepdims=True)
    own_ok = jnp.sum(jnp.where(mine, 1.0, 0.0), axis=1, keepdims=True)
    ky = (iota((1, NY), 1) - KXR).astype(F32)
    radius = own_kx * own_kx + ky * ky
    inside = jnp.where(radius <= float(KXR * KXR), 1.0, 0.0) * own_ok


    shift = BASE_SHIFT + MODE_SHIFT * (radius / float(KXR * KXR))
    for k in range(NZ):
        pivot = -(below[k] + above[k] + metric[k] * shift)
        if k > 0:
            pivot = pivot - below[k] * above[k - 1] * pivots[2, k - 1]
        pivots[0, k] = pivot
        pivots[2, k] = 1.0 / pivot
    for k in range(NZ - 1, -1, -1):
        pivot = -(below[k] + above[k] + metric[k] * shift)
        if k < NZ - 1:
            pivot = pivot - above[k] * below[k + 1] * pivots[3, k + 1]
        pivots[1, k] = pivot
        pivots[3, k] = 1.0 / pivot

    pl.semaphore_wait(meeting.at[1], 2)
    meet(2, ((0, 4), (0, -4)))

    def zero_rim(levels):
        @pl.when(gy == 0)
        def _():
            for level in levels:
                ext[:, level, 0:2] = jnp.zeros((3, 2, 16, 128), BF16)

        @pl.when(gy == NGY - 1)
        def _():
            for level in levels:
                ext[:, level, 18:20] = jnp.zeros((3, 2, 16, 128), BF16)

    def zero_level(edge, level, start, count):
        @pl.when(gz == edge)
        def _():
            for c in range(3):
                ext[c, level, start : start + count] = jnp.zeros((count, 16, 128), BF16)

    def at(c, level, row, count):
        return ext[c, level, pl.ds(row, count)].astype(F32)

    def flat_slopes(level, row, count):
        centre = [at(c, level, row, count) for c in range(3)]
        dx = [(next_x(f, True) - next_x(f, False)) * 0.5 for f in centre]
        dy = [(at(c, level, row + 1, count) - at(c, level, row - 1, count)) * 0.5 for c in range(3)]
        return dx, dy

    def slopes_z(level, row, count):
        return [(at(c, level + 1, row, count) - at(c, level - 1, row, count)) * 0.5 for c in range(3)]

    near[0].wait_recv()
    zero_level(0, 1, 2, 16)
    corners[0].start()
    corners[2].start()
    near[1].wait_recv()
    zero_level(NGZ - 1, 4, 2, 16)
    corners[1].start()
    corners[3].start()
    for copy in rims + corners:
        copy.wait_recv()
    for copy in corners:
        copy.wait_send()
    zero_level(0, 1, 0, 20)
    zero_level(NGZ - 1, 4, 0, 20)
    zero_rim((1, 2, 3, 4))

    @pl.loop(0, 18, unroll=6)
    def _(step):
        level, row, count = 2 + step // 9, 1 + 2 * lax.rem(step, 9), 2
        dx, dy = flat_slopes(level, row, count)
        grad = list(zip(dx, dy, slopes_z(level, row, count)))
        strain = {
            (i, j): grad[i][i] if i == j else 0.5 * (grad[i][j] + grad[j][i])
            for i in range(3) for j in range(i, 3)
        }
        squared = 2.0 * sum(strain[i, i] * strain[i, i] for i in range(3))
        squared = squared + 4.0 * sum(
            strain[i, j] * strain[i, j] for i in range(3) for j in range(i + 1, 3)
        )
        viscous = 2.0 * SMAG_COEF * jnp.sqrt(squared + STRAIN_FLOOR)
        for index, pair in enumerate(((2, 2), (0, 2), (1, 2), (0, 0), (0, 1), (1, 1))):
            stress[index, level - 1, pl.ds(row - 1, count)] = viscous * strain[pair]

    pl.semaphore_wait(meeting.at[2], 2)
    meet(3, ((0, 8), (0, -8)))

    @pl.loop(0, 18, unroll=6)
    def _(step):
        side, row, count = step // 9, 1 + 2 * lax.rem(step, 9), 2
        dx, dy = flat_slopes(1 + 3 * side, row, count)
        mixed = 0.5 * (dy[0] + dx[1])
        squared = 2.0 * (dx[0] * dx[0] + dy[1] * dy[1]) + 4.0 * mixed * mixed + STRAIN_FLOOR
        for index, value in enumerate((squared, dx[2], dy[2])):
            flat[index, side, pl.ds(row - 1, count)] = value

    for z in range(DEPTH):

        @pl.loop(0, 8, unroll=8)
        def _(step):
            row = 2 * step
            sign = 1.0 if z == 0 else -1.0

            def part(index, dz, dy):
                return stress[index, z + 1 + dz, pl.ds(row + 1 + dy, 2)]

            def wind(c, dz, dy):
                return at(c, z + 2 + dz, row + 2 + dy, 2)

            beside = 1 - 2 * z
            total = 0.5 * (wind(1, 0, 1) - wind(1, 0, -1) + wind(2, 1, 0) - wind(2, -1, 0))
            total = total + part(5, 0, 1) + part(5, 0, -1) + part(0, beside, 0)
            total = total - 2.0 * (part(3, 0, 0) + part(5, 0, 0) + part(0, 0, 0))
            total = total + (0.5 * sign) * (part(2, beside, 1) - part(2, beside, -1))
            odd = 0.5 * (wind(0, 0, 0) + part(4, 0, 1) - part(4, 0, -1) + sign * part(1, beside, 0))
            even = part(3, 0, 0)
            total = total + next_x(even + odd, True) + next_x(even - odd, False)
            begun[z, pl.ds(row, 2)] = total

    pl.semaphore_wait(meeting.at[3], 2)
    meet(4, ((0, 16), (0, -16)))

    for copy in far:
        copy.wait_recv()
    zero_level(0, 0, 0, 20)
    zero_level(NGZ - 1, 5, 0, 20)
    zero_rim((0, 5))

    @pl.loop(0, 18, unroll=6)
    def _(step):
        side, row, count = step // 9, 1 + 2 * lax.rem(step, 9), 2
        level = 1 + 3 * side
        dz = slopes_z(level, row, count)
        squared, dx_w, dy_w = (flat[index, side, pl.ds(row - 1, count)] for index in range(3))
        strain_x, strain_y = 0.5 * (dz[0] + dx_w), 0.5 * (dz[1] + dy_w)
        squared = squared + 2.0 * dz[2] * dz[2] + 4.0 * (strain_x * strain_x + strain_y * strain_y)
        viscous = 2.0 * SMAG_COEF * jnp.sqrt(squared)
        for index, value in enumerate((dz[2], strain_x, strain_y)):
            stress[index, level - 1, pl.ds(row - 1, count)] = viscous * value

    for z in range(DEPTH):

        @pl.loop(0, 8, unroll=8)
        def _(step):
            row = 2 * step
            sign = -1.0 if z == 0 else 1.0

            def part(index, dy):
                return stress[index, 3 * z, pl.ds(row + 1 + dy, 2)]

            odd = (0.5 * sign) * part(1, 0)
            total = begun[z, pl.ds(row, 2)] + part(0, 0)
            total = total + (0.5 * sign) * (part(2, 1) - part(2, -1))
            total = total + next_x(odd, True) - next_x(odd, False)
            high, low = split(total.reshape(32, 128))
            start = pl.multiple_of(32 * step, 32)
            source[0, pl.ds(start, 32), z * 128 : (z + 1) * 128] = high
            source[1, pl.ds(start, 32), z * 128 : (z + 1) * 128] = low

    for load in loads[4:]:
        load.wait()
    high, low = source[0], source[1]
    first = dot(x_first[0], high) + dot(x_first[0], low) + dot(x_first[1], high)
    parts = []
    for i in range(8):
        lines = first[32 * i : 32 * i + 32]
        left = jnp.concatenate(
            [
                jnp.concatenate(
                    [lines[0:16, 128 * z : 128 * z + 128], lines[16:32, 128 * z : 128 * z + 128]], 1
                )
                for z in range(DEPTH)
            ],
            0,
        )
        high, low = split(left)
        both = dot(jnp.concatenate([high, low], 0), x_second[i])
        value = both[0:32, 0:128] + both[32:64, 0:128] + both[0:32, 128:256]
        parts.append(value)
    pieces = []
    for i in range(0, 8, 2):
        one, two = parts[i], parts[i + 1]
        front = iota((32, 128), 1) < 64
        real = jnp.where(front, one, pltpu.roll(two, 64, 1))
        imag = jnp.where(front, pltpu.roll(one, 64, 1), two)
        pieces.append(jnp.concatenate([real, imag], 0))
    modes = jnp.concatenate(pieces, 1)
    high, low = split(modes)
    modes = jnp.concatenate([high, low], 0)
    slots = []
    for k in range(4):
        taken = lax.dot_general(
            chosen[k], modes, (((1,), (1,)), ((), ())), preferred_element_type=F32
        )
        slots.append(taken + pltpu.roll(taken, 64, 1))
    front = iota((256, 128), 1) < 64
    low, high = jnp.where(front, slots[0], slots[2]), jnp.where(front, slots[1], slots[3])
    largest = jnp.max(jnp.maximum(jnp.abs(low), jnp.abs(high)), axis=0, keepdims=True)
    exponent = jnp.ceil(jnp.log2(jnp.maximum(largest, 1e-30)) * 64.0) + 1.0
    scale = 32767.0 * jnp.exp2(exponent * (-1.0 / 64.0))
    low, high = (jnp.floor(v * scale + 0.5).astype(I32) for v in (low, high))
    words = (high << 16) | (low & 0xFFFF)
    for g in range(NGY):
        outgoing[g, 0:4] = words[4 * g : 4 * g + 4]
    outgoing[:, 4:5] = jnp.broadcast_to(exponent.astype(I32)[None], (NGY, 1, 128))

    pl.semaphore_wait(meeting.at[4], 2)

    def exchange(given, kept, there):
        return pltpu.make_async_remote_copy(
            src_ref=given,
            dst_ref=kept,
            send_sem=all_send,
            recv_sem=all_recv,
            device_id=(gz, there),
            device_id_type=MESH,
        )

    def away(half, k):
        return half + (k + 1) // 2 * (1 - 2 * lax.rem(k, 2))

    @pl.loop(0, NGY - 1, unroll=3)
    def _(k):
        step_z, step_y = away(4, lax.rem(k // 2, 8)), away(2, k // 16)
        there = (
            lax.rem(gy // 8 + step_z, 8) * 8
            + lax.rem(lax.rem(gy // 2, 4) + step_y, 4) * 2
            + lax.rem(gy + 1 + k, 2)
        )
        exchange(outgoing.at[there, 0:5], received.at[gy, 0:5], there).start()

    keep = pltpu.make_async_copy(outgoing.at[gy, 0:5], received.at[gy, 0:5], own_sem)
    keep.start()
    for copy in near + rims + far:
        copy.wait_send()
    keep.wait()

    others = pl.ds(0, NGY - 1)
    exchange(outgoing.at[others, 0:5], received.at[others, 0:5], gy).wait()

    low_level, high_level = DEPTH * gz, DEPTH * gz + 1
    arrived = received.reshape(NGY * 8, 128)
    exponent = arrived[pl.ds(4, NGY, stride=8), :]
    scale = jnp.exp2(exponent.astype(F32) * (1.0 / 64.0)) * (1.0 / 32767.0)
    words = [arrived[pl.ds(c, NGY, stride=8), :] for c in range(4)]
    turned = [(((w << 16) >> 16).astype(F32) * scale).T for w in words]
    turned += [((w >> 16).astype(F32) * scale).T for w in words]
    sign = jnp.where(iota((128, 128), 1) < 64, 1.0, -1.0)
    front = iota((8, 128), 1) < 64

    def edge(d, given, kept, kind):
        there = lax.rem(gz + d, NGZ)
        return pltpu.make_async_remote_copy(
            src_ref=given.at[jnp.where(there > gz, 0, 1)],
            dst_ref=kept.at[gz],
            send_sem=edge_send.at[kind, d],
            recv_sem=edge_recv.at[kind, d],
            device_id=(there, gy),
            device_id_type=MESH,
        )

    crossing = []
    for chi in range(2):
        mine = slice(8 * chi, 8 * chi + 8)
        left = jnp.concatenate(
            [
                jnp.concatenate([t[64 * chi : 64 * chi + 32], t[64 * chi + 32 : 64 * chi + 64]], 1)
                for t in turned
            ],
            0,
        )
        high, low = split(left)
        both = dot(jnp.concatenate([high, low], 0), y_first[...])
        value = both[0:256, 0:128] + both[256:512, 0:128] + both[0:256, 128:256]
        value = value.reshape(16, 16, 128)
        swapped = pltpu.roll(value, 64, 2)
        value = (value * turn[0] + swapped * turn[1]).reshape(8, 2, 16, 128)
        right = jnp.concatenate([value[:, z].reshape(128, 128) for z in range(DEPTH)], 1)
        high, low = split(right)
        by_high = dot(y_second[...], high)
        by_low = dot(y_second[0:256], low)
        both = by_high[0:256] + by_high[256:512] + by_low
        for z in range(DEPTH):
            lanes = slice(128 * z, 128 * z + 128)
            value = both[0:128, lanes] + pltpu.roll(both[128:256, lanes], 64, 1) * sign
            for pair in range(8):
                one, two = value[16 * pair : 16 * pair + 8], value[16 * pair + 8 : 16 * pair + 16]
                where = slice(128 * ((pair + 4) % 8), 128 * ((pair + 4) % 8) + 128)
                kept = inside[mine, where]
                spectrum[0, z, mine, where] = jnp.where(front, one, pltpu.roll(two, 64, 1)) * kept
                spectrum[1, z, mine, where] = jnp.where(front, pltpu.roll(one, 64, 1), two) * kept

        up = below[high_level] * pivots[2, low_level, mine]
        down = above[low_level] * pivots[3, high_level, mine]
        for side in range(2):
            near_level, far_level, weight = (1, 0, up) if side == 0 else (0, 1, down)
            values = [
                spectrum[part, near_level, mine] - weight * spectrum[part, far_level, mine]
                for part in range(2)
            ]
            largest = jnp.maximum(jnp.abs(values[0]), jnp.abs(values[1]))
            largest = jnp.maximum(jnp.max(largest, axis=1, keepdims=True), 1e-30)
            scale = 32767.0 / largest
            codes = jnp.concatenate([jnp.floor(v * scale + 0.5).astype(I32) for v in values], 0)
            edges[chi, side] = codes.astype(jnp.int16)
            steps[chi, side] = jnp.broadcast_to(largest * (1.0 / 32767.0), (8, 128))
        copies = [
            edge(d, given.at[chi], kept.at[chi], 2 * chi + kind)
            for d in (1, 3, 2)
            for kind, (given, kept) in enumerate(((edges, edge_in), (steps, steps_in)))
        ]
        for copy in copies:
            copy.start()
        edge_in[chi, gz] = jnp.zeros((16, NY), jnp.int16)
        steps_in[chi, gz] = jnp.zeros((8, 128), F32)
        crossing.append(copies)

    beneath = jnp.maximum(low_level - 1, 0)
    over = jnp.minimum(high_level + 1, NZ - 1)
    cross_up, cross_down = below[high_level], above[low_level]
    for chi in range(2):
        mine = slice(8 * chi, 8 * chi + 8)
        first_pivot, last_pivot = pivots[0, low_level, mine], pivots[1, high_level, mine]
        inverse = 1.0 / (first_pivot * last_pivot - cross_up * cross_down)
        from_below = below[low_level] * pivots[2, beneath, mine]
        from_above = above[high_level] * pivots[3, over, mine]
        for copy in crossing[chi]:
            copy.wait()

        def edges_of(block):
            step = jnp.concatenate([steps_in[chi, block]] * (NY // 128), 1)
            codes = edge_in[chi, block].astype(I32).astype(F32)
            return codes[0:8] * step, codes[8:16] * step

        arriving = [edges_of(block) for block in range(NGZ)]
        for part in range(2):
            reached = jnp.zeros((8, NY), F32)
            for block in range(NGZ - 1):
                new = arriving[block][part]
                if block > 0:
                    k = DEPTH * block
                    along = pivots[2, k - 1, mine] * pivots[2, k, mine]
                    new = new + (below[k] * below[k + 1]) * along * reached
                reached = jnp.where(block < gz, new, reached)
            lower = spectrum[part, 0, mine] - from_below * reached
            reached = jnp.zeros((8, NY), F32)
            for block in range(NGZ - 1, 0, -1):
                new = arriving[block][part]
                if block < NGZ - 1:
                    k = DEPTH * block
                    along = pivots[3, k + 1, mine] * pivots[3, k + 2, mine]
                    new = new + (above[k] * above[k + 1]) * along * reached
                reached = jnp.where(block > gz, new, reached)
            upper = spectrum[part, 1, mine] - from_above * reached
            for z, value in enumerate(
                (last_pivot * lower - cross_down * upper, first_pivot * upper - cross_up * lower)
            ):
                value = value * inverse
                for tile in range(NY // 128):
                    out[pl.ds(256 * chi + part * 16 + tile * 2 + z, 8, stride=32), :] = value[
                        :, tile * 128 : (tile + 1) * 128
                    ]


def per_device(velocity_x, velocity_y, velocity_z, owners, below, above, metric):
    anywhere = pl.BlockSpec(memory_space=pl.ANY)
    scalars = pl.BlockSpec(memory_space=pltpu.SMEM)
    consts = [jnp.asarray(t) for t in tables()]
    dma = pltpu.SemaphoreType.DMA
    result = pl.pallas_call(
        kernel,
        out_shape=pltpu.VMEM((2 * DEPTH * CAP * NY // 128, 128), F32),
        in_specs=[anywhere] * 4 + [scalars] * 3 + [anywhere] * 5,
        out_specs=pl.BlockSpec(memory_space=pltpu.VMEM),
        scratch_shapes=[
            pltpu.VMEM((3, DEPTH, ROWS, NX), BF16),
            pltpu.VMEM((1, KXR), I32),
            pltpu.VMEM((3 * DEPTH * ROWS * 16, 128), F32),
            pltpu.VMEM((3, 6, 20, 16, 128), BF16),
            pltpu.VMEM((6, 4, 18, 16, 128), F32),
            pltpu.VMEM((3, 2, 18, 16, 128), F32),
            pltpu.VMEM((DEPTH, ROWS, 16, 128), F32),
            pltpu.VMEM((2, 256, 256), BF16),
            pltpu.VMEM((NGY, 8, 128), I32),
            pltpu.VMEM((NGY, 8, 128), I32),
        ]
        + [pltpu.VMEM(c.shape, c.dtype) for c in consts]
        + [
            pltpu.VMEM((4, 256, KXR), BF16),
            pltpu.VMEM((4, NZ, CAP, NY), F32),
            pltpu.VMEM((2, 2, 16, NY), jnp.int16),
            pltpu.VMEM((2, NGZ, 16, NY), jnp.int16),
            pltpu.VMEM((2, 2, 8, 128), F32),
            pltpu.VMEM((2, NGZ, 8, 128), F32),
            pltpu.VMEM((2, DEPTH, CAP, NY), F32),
            dma((9,)), dma((14,)), dma((14,)), dma(()), dma(()), dma((4, NGZ)), dma((4, NGZ)),
            dma(()),
            pltpu.SemaphoreType.REGULAR((5,)),
        ],
        compiler_params=pltpu.CompilerParams(collective_id=0, has_side_effects=True),
    )(velocity_x, velocity_y, velocity_z, owners.reshape(1, KXR), below, above, metric, *consts)
    result = result.reshape(CAP, 2, NY // 128, DEPTH, 128)
    return jnp.transpose(result, (0, 1, 3, 2, 4)).reshape(1, CAP, 2, DEPTH, NY)


def solution(mesh):
    placed = (P("gz", "gy", None), P("gz", "gy", None), P("gz", "gy", None), P(), P(), P(), P())
    return jax.shard_map(
        per_device,
        mesh=mesh,
        in_specs=placed,
        out_specs=P("gy", None, None, "gz", None),
        check_vma=False,
    )
```
